32 devices in a mesh: ia: 2 (over x), ja: 4 (over z), ka: 4 (over y, core).
Axes of the slice: x: 2, y: 2, z: 4, core: 2. Of those that a mesh axis runs over, the one named last changes fastest.
Arguments:
- flow_state: float32 [5, 4, 64, 64, 128], P(None, 'ka', 'ia', 'ja'), may hold values from -6 to 6
- spectral: float32 [3, 4, 64, 64, 128], P(None, 'ka', 'ia', 'ja'), may hold values from 0.5 to 50
- wave_speed: float32 [3, 4, 5], P(None, 'ka'), may hold values from 0.05 to 2
- left_map: float32 [4, 5, 5], P('ka')
- right_map: float32 [4, 5, 5], P('ka')
- donor_block: int32 [32, 32, 1], P(('ia', 'ja', 'ka')), may hold values from 0 to 127
- receiver_block: int32 [32, 32, 1], P(('ia', 'ja', 'ka')), may hold values from 0 to 127, as said below
- fringe_count: int32 [32, 32], P(('ia', 'ja', 'ka')), may hold values from 0 to 1, as said below
- fringe_weight: float32 [3, 32, 32, 1], P(None, ('ia', 'ja', 'ka')), may hold values from 0 to 1
Outputs:
- advanced: float32 [5, 4, 64, 64, 128], P(None, 'ka', 'ia', 'ja')
- increment: float32 [5, 4, 64, 64, 128], P(None, 'ka', 'ia', 'ja')
The draws below stay inside these ranges and needn't reach their ends.
Inputs may be any that keep to these rules, and one draw needn't show every extreme that they name: `receiver_block`: on each receiving device the cube numbers over all sources and slots are distinct. `fringe_count`: in every draw some receiving device has 1 live slots from every source.
All inputs are finite; a program needn't handle non-finite values.
Results may differ from the reference program's by a relative error of at most 0.0003.
Values sent between devices are 32-bit elements; how exact they have to be, the bound alone decides.
A program may use at most 128 MiB of HBM per device.

```python
import jax
import jax.numpy as jnp
from jax import lax

V = 5
GRID_DEV = 1
CI = 32
CJ = 16
NK = 128
BS = 8
CAP = 1
GRIDS = 4
NI = 64
NJ = 64
BLK_DEV = 128
N_IA = 2
N_JA = 4
N_KA = 4


def transform_draw(key):
    noise = jax.random.uniform(key, (GRIDS, V, V), jnp.float32, -0.3, 0.3)
    diagonal = (jnp.arange(V)[:, None] == jnp.arange(V)[None, :]).astype(jnp.float32)
    return diagonal + noise


def draw_left_map(key, part):
    return transform_draw(jax.random.fold_in(key, 11))


def draw_right_map(key, part):
    return transform_draw(jax.random.fold_in(key, 23))


def draw_spectral(key, part):
    unit = jax.random.uniform(jax.random.fold_in(key, 31), (3, GRIDS, NI, NJ, NK), jnp.float32)
    lower = jnp.full((3, 1, 1, 1, 1), 0.5, jnp.float32)
    upper = jnp.full((3, 1, 1, 1, 1), 50.0, jnp.float32)
    return jnp.exp(jnp.log(lower) + unit * (jnp.log(upper) - jnp.log(lower)))


def draw_wave_speed(key, part):
    unit = jax.random.uniform(jax.random.fold_in(key, 37), (3, GRIDS, V), jnp.float32)
    speeds = jnp.exp(jnp.log(0.05) + unit * (jnp.log(2.0) - jnp.log(0.05)))
    return speeds


def draw_fringe_count(key, part):
    devices = N_IA * N_JA * N_KA
    counts = jax.random.randint(jax.random.fold_in(key, 1), (devices, devices), 0, CAP + 1)
    heavy = jax.random.randint(jax.random.fold_in(key, 2), (), 0, devices)
    receivers = jnp.arange(devices)[:, None]
    senders = jnp.arange(devices)[None, :]
    counts = jnp.where(receivers == heavy, CAP, counts)
    counts = jnp.where(senders == (receivers + 1) % devices, CAP, counts)
    return counts.astype(jnp.int32)


def permute_one(subkey):
    return jax.random.permutation(subkey, BLK_DEV)


def draw_receiver_block(key, part):
    devices = N_IA * N_JA * N_KA
    subkeys = jax.random.split(jax.random.fold_in(key, 5), devices)
    orders = jax.vmap(permute_one)(subkeys)
    return orders[:, :devices * CAP].reshape(devices, devices, CAP).astype(jnp.int32)


def place_ends(result, stream_key, least, high):
    index_at = [jax.random.randint(jax.random.fold_in(stream_key, axis), (), 0, length) for axis, length in enumerate(result.shape)]
    main_axis = result.shape.index(max(result.shape))
    neighbour = index_at[:main_axis] + [(index_at[main_axis] + 1) % result.shape[main_axis]] + index_at[main_axis + 1:]
    return result.at[tuple(index_at)].set(least).at[tuple(neighbour)].set(high)


def shard_levels(rng, shape, cuts, low, largest):
    gain = 1.0
    for dim, parts in cuts:
        steps = jax.random.uniform(jax.random.fold_in(jax.random.fold_in(rng, 6), dim), (parts,), jnp.float32, low / len(cuts), largest / len(cuts))
        gain = gain * jnp.repeat(jnp.exp(steps), shape[dim] // parts).reshape((-1,) + (1,) * (len(shape) - 1 - dim))
    return gain


def normal_values(key, extent, deviation, limit, cuts=(), kind=jnp.bfloat16):
    entries = jax.random.normal(key, extent, jnp.float32) * deviation
    if len(cuts) > 0:
        entries = shard_levels(key, extent, cuts, -0.22, 0.18) * entries
    return jnp.clip(entries, min=-limit, max=limit).astype(kind)


def setup_inputs(seed: int = 0) -> dict:
    keys = jax.random.split(jax.random.key(seed), 10)
    return {
        "flow_state": normal_values(keys[0], (V, GRIDS, NI, NJ, NK), 1.0, 6.0, ((1, 4), (2, 2), (3, 4)), jnp.float32),
        "spectral": draw_spectral(jax.random.fold_in(keys[9], 71), 0),
        "wave_speed": draw_wave_speed(jax.random.fold_in(keys[9], 71), 0),
        "left_map": draw_left_map(jax.random.fold_in(keys[9], 71), 0),
        "right_map": draw_right_map(jax.random.fold_in(keys[9], 71), 0),
        "donor_block": place_ends(jax.random.randint(keys[5], (N_IA * N_JA * N_KA, N_IA * N_JA * N_KA, CAP), 0, BLK_DEV), jax.random.fold_in(keys[5], 1), 0, BLK_DEV - 1).astype(jnp.int32),
        "receiver_block": draw_receiver_block(jax.random.fold_in(keys[9], 71), 0),
        "fringe_count": draw_fringe_count(jax.random.fold_in(keys[9], 71), 0),
        "fringe_weight": jnp.clip(1.0 * jax.random.uniform(keys[8], (3, N_IA * N_JA * N_KA, N_IA * N_JA * N_KA, CAP), jnp.float32) ** shard_levels(keys[8], (3, N_IA * N_JA * N_KA, N_IA * N_JA * N_KA, CAP), ((1, 32),), -0.2, 0.2), 0.0, 1.0),
    }


QUARTER = 0.25


def forward_step(carried, inputs):
    older_first, older_second, older_value, last_first, last_second, last_value = carried
    source, coupling = inputs
    fourth = QUARTER * coupling
    coupled = -coupling + fourth * older_first
    pivots = 1.0 + 2.0 * coupling + 2.0 * fourth + fourth * older_second - last_first * coupled
    first_gain = (-coupling - last_second * coupled) / pivots
    second_gain = -fourth / pivots
    reduced = (source + fourth * older_value - coupled * last_value) / pivots
    return (last_first, last_second, last_value, first_gain, second_gain, reduced), (first_gain, second_gain, reduced)


def backward_step(carried, inputs):
    next_value, after_next = carried
    first_gain, second_gain, reduced = inputs
    solved = reduced - first_gain * next_value - second_gain * after_next
    return (solved, next_value), solved


def solve_lines(source, coupling):
    zeros_plane = jnp.zeros(source.shape[1:], jnp.float32)
    ignored, factors = lax.scan(forward_step, (zeros_plane,) * 6, (source, coupling))
    ignored, solved = lax.scan(backward_step, (zeros_plane, zeros_plane), factors, reverse=True)
    return solved


def blend_axis(blocks, weight, along_dim):
    size_along = blocks.shape[along_dim]
    shifted = jnp.concatenate([lax.slice_in_dim(blocks, 1, size_along, axis=along_dim), lax.slice_in_dim(blocks, size_along - 1, size_along, axis=along_dim)], axis=along_dim)
    return (1.0 - weight) * blocks + weight * shifted


def interpolate(blocks, weights):
    expanded = weights[..., None, None, None, None]
    blocks = blend_axis(blocks, expanded[0], blocks.ndim - 3)
    blocks = blend_axis(blocks, expanded[1], blocks.ndim - 2)
    return blend_axis(blocks, expanded[2], blocks.ndim - 1)


def to_cubes(field):
    shaped = field.reshape(V, N_KA, GRID_DEV, N_IA, CI // BS, BS, N_JA, CJ // BS, BS, NK // BS, BS)
    ordered = shaped.transpose(3, 6, 1, 2, 4, 7, 9, 0, 5, 8, 10)
    return ordered.reshape(N_IA * N_JA * N_KA, BLK_DEV, V * BS ** 3)


def from_cubes(cube_rows):
    shaped = cube_rows.reshape(N_IA, N_JA, N_KA, GRID_DEV, CI // BS, CJ // BS, NK // BS, V, BS, BS, BS)
    return shaped.transpose(7, 2, 3, 0, 4, 8, 1, 5, 9, 6, 10).reshape(V, GRIDS, NI, NJ, NK)


def place_cubes(device_cubes, device_target, device_values):
    return device_cubes.at[device_target].set(device_values, mode="drop")


def grid_step(inputs):
    residual, spectral, speeds, left_grid, right_grid = inputs
    characteristic = jnp.einsum("vu,uijk->vijk", left_grid, residual, precision=lax.Precision.HIGHEST)
    moved = jnp.moveaxis(characteristic, 1, 0)
    coupling = speeds[0][None, :, None, None] * spectral[0][:, None, :, :]
    characteristic = jnp.moveaxis(solve_lines(moved, coupling), 0, 1)
    moved = jnp.moveaxis(characteristic, 2, 0)
    coupling = speeds[1][None, :, None, None] * jnp.moveaxis(spectral[1], 1, 0)[:, None, :, :]
    characteristic = jnp.moveaxis(solve_lines(moved, coupling), 0, 2)
    moved = jnp.moveaxis(characteristic, 3, 0)
    coupling = speeds[2][None, :, None, None] * jnp.moveaxis(spectral[2], 2, 0)[:, None, :, :]
    characteristic = jnp.moveaxis(solve_lines(moved, coupling), 0, 3)
    return jnp.einsum("vu,uijk->vijk", right_grid, characteristic, precision=lax.Precision.HIGHEST)


def reference(flow_state, spectral, wave_speed, left_map, right_map, donor_block, receiver_block, fringe_count, fringe_weight):
    devices = N_IA * N_JA * N_KA
    cube_rows = to_cubes(flow_state)
    sources = jnp.arange(devices, dtype=jnp.int32)
    outbound = cube_rows[sources[:, None, None], donor_block]
    arrived = jnp.swapaxes(outbound, 0, 1)
    blocks = arrived.reshape(devices, devices, CAP, V, BS, BS, BS)
    blended = interpolate(blocks, fringe_weight)
    live_slot = jnp.arange(CAP, dtype=jnp.int32)[None, None, :] < fringe_count[:, :, None]
    target = jnp.where(live_slot, receiver_block, BLK_DEV).astype(jnp.int32)
    cube_rows = jax.vmap(place_cubes)(cube_rows, target.reshape(devices, devices * CAP), blended.reshape(devices, devices * CAP, V * BS ** 3))
    filled = from_cubes(cube_rows)
    padded = jnp.pad(filled, ((0, 0), (0, 0), (1, 1), (1, 1), (1, 1)))
    center = filled
    along_i = padded[:, :, 2:, 1:-1, 1:-1] + padded[:, :, :-2, 1:-1, 1:-1] - 2.0 * center
    along_j = padded[:, :, 1:-1, 2:, 1:-1] + padded[:, :, 1:-1, :-2, 1:-1] - 2.0 * center
    along_k = padded[:, :, 1:-1, 1:-1, 2:] + padded[:, :, 1:-1, 1:-1, :-2] - 2.0 * center
    residual = spectral[0][None] * along_i + spectral[1][None] * along_j + spectral[2][None] * along_k
    per_grid = (jnp.swapaxes(residual, 0, 1), jnp.swapaxes(spectral, 0, 1), jnp.swapaxes(wave_speed, 0, 1), left_map, right_map)
    increment = jnp.swapaxes(lax.map(grid_step, per_grid), 0, 1)
    return filled + increment, increment
```

```python
import functools

import jax
import jax.numpy as jnp
from jax import lax
from jax.experimental import pallas as pl
from jax.experimental.pallas import tpu as pltpu
from jax.sharding import PartitionSpec as P

BS = 8
LANES = 128
GROUPS = LANES // BS
QUARTER = 0.25
VMEM = pl.BlockSpec(memory_space=pltpu.VMEM)
SMEM = pl.BlockSpec(memory_space=pltpu.SMEM)
F32 = jnp.float32


def call(body, outs, ins, args, scratch=(), flops=4_000_000):
    moved = sum(a.size * 4 for a in args) + sum(o.size * 4 for o in outs)
    return pl.pallas_call(
        body,
        out_shape=outs,
        in_specs=ins,
        out_specs=[VMEM] * len(outs),
        scratch_shapes=list(scratch),
        compiler_params=pltpu.CompilerParams(vmem_limit_bytes=40 << 20),
        cost_estimate=pl.CostEstimate(flops=flops, bytes_accessed=moved, transcendentals=0),
    )(*args)


def shape(*dims):
    return jax.ShapeDtypeStruct(dims, F32)


def lane_iota():
    return lax.broadcasted_iota(jnp.int32, (BS, LANES), 1)


def split_block(block, blocks_j):
    along_k = block % GROUPS
    rest = block // GROUPS
    return rest // blocks_j, rest % blocks_j, along_k


def pack_body(rows_j, donor, flow, outbound):
    variables = flow.shape[0]
    group = lane_iota() // BS

    def one(slot, carry):
        block_i, block_j, block_k = split_block(donor[slot], rows_j // BS)
        first = block_i * (BS * rows_j) + block_j * BS
        tiles = [jnp.zeros((BS, LANES), F32) for q in range(outbound.shape[1] // BS)]
        for g in range(variables * BS):
            row = pl.multiple_of(first + (g % BS) * rows_j, BS)
            tile = flow[g // BS, pl.ds(row, BS), :]
            moved = pltpu.roll(tile, (g * BS - block_k * BS + 8 * LANES) % LANES, 1)
            tiles[g // GROUPS] = jnp.where(group == g % GROUPS, moved, tiles[g // GROUPS])
        for q, tile in enumerate(tiles):
            outbound[slot, q * BS : (q + 1) * BS, :] = tile
        return carry

    lax.fori_loop(0, outbound.shape[0], one, 0)


def blend(cubes, shifted, weight):
    return (1.0 - weight) * cubes + weight * shifted


def fill_body(
    rows_j, capacity, receiver, count, weights, flow, arrived, filled, i_low, i_high, j_low, j_high
):
    variables = flow.shape[0]
    slots, packed_rows, lanes = arrived.shape
    group = lane_iota() // BS
    lane = lax.broadcasted_iota(jnp.int32, (packed_rows, LANES), 1)
    row = lax.broadcasted_iota(jnp.int32, (packed_rows, LANES), 0)
    filled[...] = flow[...]

    def one(slot, carry):
        @pl.when(slot % capacity < count[slot // capacity])
        def _():
            cubes = arrived[slot]
            after = jnp.where(lane % (BS * BS) >= BS * (BS - 1), cubes, pltpu.roll(cubes, LANES - BS, 1))
            cubes = blend(cubes, after, weights[slot])
            after = jnp.where(row % BS == BS - 1, cubes, pltpu.roll(cubes, packed_rows - 1, 0))
            cubes = blend(cubes, after, weights[slots + slot])
            after = jnp.where(lane % BS == BS - 1, cubes, pltpu.roll(cubes, LANES - 1, 1))
            cubes = blend(cubes, after, weights[2 * slots + slot])
            block_i, block_j, block_k = split_block(receiver[slot], rows_j // BS)
            first = block_i * (BS * rows_j) + block_j * BS
            here = group == block_k
            for g in range(variables * BS):
                q = g // GROUPS
                tile = cubes[q * BS : (q + 1) * BS]
                moved = pltpu.roll(tile, (block_k * BS - g * BS + 8 * LANES) % LANES, 1)
                at = pl.ds(pl.multiple_of(first + (g % BS) * rows_j, BS), BS)
                filled[g // BS, at, :] = jnp.where(here, moved, filled[g // BS, at, :])

        return carry

    lax.fori_loop(0, slots, one, 0)
    rows_i = flow.shape[1] // rows_j
    for v in range(variables):
        i_low[v] = filled[v, :rows_j, :]
        i_high[v] = filled[v, (rows_i - 1) * rows_j :, :]
        j_low[v] = filled[v, pl.ds(0, rows_i, stride=rows_j), :]
        j_high[v] = filled[v, pl.ds(rows_j - 1, rows_i, stride=rows_j), :]


def eliminate(coupling, older_first, older_second, last_first, last_second):
    fourth = QUARTER * coupling
    coupled = -coupling + fourth * older_first
    pivots = 1.0 + 2.5 * coupling + fourth * older_second - last_first * coupled
    inverse = 1.0 / pivots
    first = (-coupling - last_second * coupled) * inverse
    second = -fourth * inverse
    return inverse, coupled * inverse, first, second


def meet(gains, values, far_gains, far_values):
    f0, s0, f1, s1 = gains
    g0, t0, g1, t1 = far_gains
    r0, r1 = values
    q0, q1 = far_values
    cross = g1 - t1 * f0
    a11 = 1.0 - t1 * s0 - cross * f1
    a12 = -cross * s1
    b1 = q1 - t1 * r0 - cross * r1
    a21 = g0 - t0 * f1
    a22 = 1.0 - t0 * s1
    b2 = q0 - t0 * r1
    scale = 1.0 / (a11 * a22 - a12 * a21)
    return (b1 * a22 - a12 * b2) * scale, (a11 * b2 - a21 * b1) * scale


def row_of(n, count, lower):
    return jnp.where(lower, n, count - 1 - n)


def factor_body(direction, rows, stride, lower, speeds, spectral, start, inverse, coupled, first, second, last):
    variables, total, lanes = inverse.shape
    plane = total // rows
    is_lower = lower[0] == 1

    def one(n, carry):
        row = row_of(n, rows, is_lower)
        at = pl.ds(pl.multiple_of(row * plane, BS), plane)
        if stride is None:
            rho = spectral[direction, at, :]
        else:
            rho = spectral[direction, pl.ds(row, plane, stride=stride), :]
        fresh = []
        for v in range(variables):
            older_first, older_second, last_first, last_second = carry[v]
            a, b, c, d = eliminate(
                speeds[direction * variables + v] * rho, older_first, older_second, last_first, last_second
            )
            inverse[v, at, :] = a
            coupled[v, at, :] = b
            first[v, at, :] = c
            second[v, at, :] = d
            fresh.append((last_first, last_second, c, d))
        return tuple(fresh)

    begin = tuple(tuple(start[m, v] for m in range(4)) for v in range(variables))
    ends = lax.fori_loop(0, rows, one, begin)
    for v in range(variables):
        for m in range(4):
            last[m, v] = ends[v][m]


def residual_body(
    rows_i, lower, left, filled, spectral, i_before, i_after, j_before, j_after,
    inverse, coupled, second, reduced, last, padded,
):
    variables, total, lanes = filled.shape
    rows_j = total // rows_i
    is_lower = lower[0] == 1
    padded[:, :rows_j, :] = i_before[...]
    padded[:, rows_j : rows_j + total, :] = filled[...]
    padded[:, rows_j + total :, :] = i_after[...]
    lane = lax.broadcasted_iota(jnp.int32, (rows_j, lanes), 1)
    row_id = lax.broadcasted_iota(jnp.int32, (rows_j, lanes), 0)

    def one(n, carry):
        row = row_of(n, rows_i, is_lower)
        base = pl.multiple_of(row * rows_j, BS)
        at = pl.ds(base, rows_j)
        rho = [spectral[e, at, :] for e in range(3)]
        residual = []
        for v in range(variables):
            center = padded[v, pl.ds(base + rows_j, rows_j), :]
            twice = 2.0 * center
            along_i = padded[v, pl.ds(base + 2 * rows_j, rows_j), :] + padded[v, at, :] - twice
            after = jnp.where(
                row_id == rows_j - 1, j_after[v, pl.ds(row, 1), :], pltpu.roll(center, rows_j - 1, 0)
            )
            before = jnp.where(row_id == 0, j_before[v, pl.ds(row, 1), :], pltpu.roll(center, 1, 0))
            along_j = after + before - twice
            after = jnp.where(lane == lanes - 1, 0.0, pltpu.roll(center, lanes - 1, 1))
            before = jnp.where(lane == 0, 0.0, pltpu.roll(center, 1, 1))
            along_k = after + before - twice
            residual.append(rho[0] * along_i + rho[1] * along_j + rho[2] * along_k)
        fresh = []
        for v in range(variables):
            source = left[v * variables] * residual[0]
            for u in range(1, variables):
                source = source + left[v * variables + u] * residual[u]
            older, newer = carry[v]
            value = source * inverse[v, at, :] - second[v, at, :] * older - coupled[v, at, :] * newer
            reduced[v, at, :] = value
            fresh.append((newer, value))
        return tuple(fresh)

    last[...] = jnp.zeros(last.shape, F32)
    ends = lax.fori_loop(0, rows_i, one, begin_of(last, variables))
    for v in range(variables):
        last[0, v] = ends[v][0]
        last[1, v] = ends[v][1]


def forward_body(rows, lower, source, inverse, coupled, second, start, reduced, last):
    variables, total, lanes = source.shape
    plane = total // rows
    is_lower = lower[0] == 1

    def one(n, carry):
        at = pl.ds(pl.multiple_of(row_of(n, rows, is_lower) * plane, BS), plane)
        fresh = []
        for v in range(variables):
            older, newer = carry[v]
            value = (
                source[v, at, :] * inverse[v, at, :]
                - second[v, at, :] * older
                - coupled[v, at, :] * newer
            )
            reduced[v, at, :] = value
            fresh.append((newer, value))
        return tuple(fresh)

    begin = tuple((start[0, v], start[1, v]) for v in range(variables))
    ends = lax.fori_loop(0, rows, one, begin)
    for v in range(variables):
        last[0, v] = ends[v][0]
        last[1, v] = ends[v][1]


def backward_pass(rows, is_lower, reduced, first, second, begin, store):
    variables, total, lanes = reduced.shape
    plane = total // rows

    def one(step, carry):
        row = row_of(rows - 1 - step, rows, is_lower)
        at = pl.ds(pl.multiple_of(row * plane, BS), plane)
        fresh = []
        for v in range(variables):
            nearer, farther = carry[v]
            value = reduced[v, at, :] - first[v, at, :] * nearer - second[v, at, :] * farther
            store(v, row, value)
            fresh.append((value, nearer))
        return tuple(fresh)

    return lax.fori_loop(0, rows, one, begin)


def start_values(variables, gains, values, far_gains, far_values):
    return tuple(
        meet(
            [gains[m, v] for m in range(4)],
            [values[m, v] for m in range(2)],
            [far_gains[m, v] for m in range(4)],
            [far_values[m, v] for m in range(2)],
        )
        for v in range(variables)
    )


def begin_of(next_values, variables):
    return tuple((next_values[0, v], next_values[1, v]) for v in range(variables))


def first_solved_body(rows, lower, reduced, first, second, next_values, solved):
    variables = reduced.shape[0]
    ends = backward_pass(
        rows, lower[0] == 1, reduced, first, second, begin_of(next_values, variables), lambda v, row, x: None
    )
    for v in range(variables):
        solved[0, v] = ends[v][0]
        solved[1, v] = ends[v][1]


def meet_body(gains, values, far_gains, far_values, next_values):
    variables = gains.shape[1]
    for v, pair in enumerate(start_values(variables, gains, values, far_gains, far_values)):
        next_values[0, v] = pair[0]
        next_values[1, v] = pair[1]


def turn_body(rows_i, lower, reduced, first, second, next_values, turned):
    variables, total, lanes = reduced.shape
    rows_j = total // rows_i

    def store(v, row, value):
        turned[v, pl.ds(row, rows_j, stride=rows_i), :] = value

    backward_pass(
        rows_i, lower[0] == 1, reduced, first, second, begin_of(next_values, variables), store
    )


def finish_body(
    rows_j, lower, speeds, right, reduced, first, second, next_values, spectral, filled,
    advanced, increment, lines, values, coupling, gain_1, gain_2,
):
    variables, total, lanes = reduced.shape
    rows_i = total // rows_j
    quarters = total // LANES
    per_quarter = LANES // rows_i
    depth = values.shape[0] // lanes

    def store(v, row, value):
        lines[v, pl.ds(pl.multiple_of(row * rows_i, BS), rows_i), :] = value

    backward_pass(
        rows_j, lower[0] == 1, reduced, first, second, begin_of(next_values, variables), store
    )
    for q in range(quarters):
        rho = jnp.concatenate(
            [
                spectral[2, pl.ds(q * per_quarter + j, rows_i, stride=rows_j), :]
                for j in range(per_quarter)
            ],
            axis=0,
        ).T
        for v in range(variables):
            at = pl.ds(v * quarters + q, lanes, stride=depth)
            coupling[at, :] = speeds[2 * variables + v] * rho
            values[at, :] = lines[v, q * LANES : (q + 1) * LANES, :].T
    for spare in range(variables * quarters, depth):
        at = pl.ds(spare, lanes, stride=depth)
        coupling[at, :] = jnp.zeros((lanes, lanes), F32)
        values[at, :] = jnp.zeros((lanes, lanes), F32)

    half = lanes // 2
    gain_1[:depth, :] = jnp.zeros((depth, lanes), F32)
    zero = gain_1[:depth, :]

    def ahead(n, carry):
        fresh = []
        for side in range(2):
            older_first, older_second, older, last_first, last_second, newer = carry[side]
            k = n if side == 0 else lanes - 1 - n
            at = pl.ds(pl.multiple_of(k * depth, BS), depth)
            inverse, coupled, one, two = eliminate(
                coupling[at, :], older_first, older_second, last_first, last_second
            )
            value = values[at, :] * inverse - two * older - coupled * newer
            gain_1[at, :] = one
            gain_2[at, :] = two
            values[at, :] = value
            fresh.append((last_first, last_second, newer, one, two, value))
        return tuple(fresh)

    low, high = lax.fori_loop(0, half, ahead, ((zero,) * 6,) * 2)

    def ends(side):
        return [side[0], side[1], side[3], side[4]], [side[2], side[5]]

    low_next = meet(*ends(low), *ends(high))
    high_next = meet(*ends(high), *ends(low))

    def back(step, carry):
        fresh = []
        for side in range(2):
            nearer, farther = carry[side]
            n = half - 1 - step
            k = n if side == 0 else lanes - 1 - n
            at = pl.ds(pl.multiple_of(k * depth, BS), depth)
            value = values[at, :] - gain_1[at, :] * nearer - gain_2[at, :] * farther
            values[at, :] = value
            fresh.append((value, nearer))
        return tuple(fresh)

    lax.fori_loop(0, half, back, (low_next, high_next))
    for q in range(quarters):
        solved = [values[pl.ds(u * quarters + q, lanes, stride=depth), :] for u in range(variables)]
        for v in range(variables):
            total_v = right[v * variables] * solved[0]
            for u in range(1, variables):
                total_v = total_v + right[v * variables + u] * solved[u]
            turned = total_v.T
            for j in range(per_quarter):
                at = pl.ds(q * per_quarter + j, rows_i, stride=rows_j)
                piece = turned[j * rows_i : (j + 1) * rows_i]
                increment[v, at, :] = piece
                advanced[v, at, :] = filled[v, at, :] + piece


def routes(axis):
    members = lax.axis_size(axis)
    assert members % 2 == 0
    half = members // 2
    inward = [(d, d + 1) for d in range(half - 1)] + [(d, d - 1) for d in range(half + 1, members)]
    outward = [(b, a) for a, b in inward]
    across = [(half - 1, half), (half, half - 1)]
    place = lax.axis_index(axis)
    middle = (place == half - 1) | (place == half)
    lower = (place < half).astype(jnp.int32).reshape(1)
    return half, inward, outward, across, middle, lower


def local(
    flow_state, spectral, wave_speed, left_map, right_map,
    donor_block, receiver_block, fringe_count, fringe_weight,
):
    variables, grids, rows_i, rows_j, rows_k = flow_state.shape
    assert grids == 1 and rows_k == LANES
    total = rows_i * rows_j
    devices, capacity = donor_block.shape[1:]
    slots = devices * capacity
    flow = flow_state.reshape(variables, total, rows_k)
    rho = spectral.reshape(3, total, rows_k)
    speeds = wave_speed.reshape(-1)
    left = left_map.reshape(-1)
    right = right_map.reshape(-1)
    packed_rows = -(-variables * BS // GROUPS) * BS
    half_i, in_i, out_i, across_i, middle_i, lower_i = routes("ia")
    half_j, in_j, out_j, across_j, middle_j, lower_j = routes("ja")
    field = shape(variables, total, rows_k)
    i_plane = (variables, rows_j, rows_k)
    j_plane = (variables, rows_i, rows_k)

    (outbound,) = call(
        functools.partial(pack_body, rows_j),
        [shape(slots, packed_rows, LANES)],
        [SMEM, VMEM],
        (donor_block.reshape(-1), flow),
    )
    arrived = lax.all_to_all(outbound, ("ia", "ja", "ka"), split_axis=0, concat_axis=0, tiled=True)

    def factors(direction, axis, rows, stride, plane, half, inward, across, lower):
        start = jnp.zeros((4,) + plane, F32)
        for hop in range(half):
            *gains, last = call(
                functools.partial(factor_body, direction, rows, stride),
                [field] * 4 + [shape(4, *plane)],
                [SMEM, SMEM, VMEM, VMEM],
                (lower, speeds, rho, start),
            )
            if hop < half - 1:
                start = lax.ppermute(last, axis, inward)
        return gains, last, lax.ppermute(last, axis, across)

    gains_i, last_i, far_i = factors(0, "ia", rows_i, None, i_plane, half_i, in_i, across_i, lower_i)
    gains_j, last_j, far_j = factors(1, "ja", rows_j, rows_j, j_plane, half_j, in_j, across_j, lower_j)

    filled, i_low, i_high, j_low, j_high = call(
        functools.partial(fill_body, rows_j, capacity),
        [field, shape(*i_plane), shape(*i_plane), shape(*j_plane), shape(*j_plane)],
        [SMEM, SMEM, SMEM, VMEM, VMEM],
        (receiver_block.reshape(-1), fringe_count.reshape(-1), fringe_weight.reshape(-1), flow, arrived),
    )

    def beside(low, high, axis):
        members = lax.axis_size(axis)
        up = [(d, d + 1) for d in range(members - 1)]
        return lax.ppermute(high, axis, up), lax.ppermute(low, axis, [(b, a) for a, b in up])

    i_before, i_after = beside(i_low, i_high, "ia")
    j_before, j_after = beside(j_low, j_high, "ja")

    inverse, coupled, first, second = gains_i
    reduced, last = call(
        functools.partial(residual_body, rows_i),
        [field, shape(2, *i_plane)],
        [SMEM, SMEM] + [VMEM] * 9,
        (lower_i, left, filled, rho, i_before, i_after, j_before, j_after, inverse, coupled, second),
        scratch=[pltpu.VMEM((variables, total + 2 * rows_j, rows_k), F32)],
    )

    def inner_values(last_gains, far_gains, last, axis, across):
        far = lax.ppermute(last, axis, across)
        (values,) = call(
            meet_body,
            [shape(*last.shape)],
            [VMEM] * 4,
            (last_gains, last, far_gains, far),
        )
        return values

    def outer_values(values, rows, half, outward, middle, axis, lower, reduced, first, second):
        inner = values
        for hop in range(half - 1):
            (solved,) = call(
                functools.partial(first_solved_body, rows),
                [shape(*values.shape)],
                [SMEM] + [VMEM] * 4,
                (lower, reduced, first, second, values),
            )
            values = jnp.where(middle, inner, lax.ppermute(solved, axis, outward))
        return values

    def sweep(source, reduced, last, gains, last_gains, far_gains, rows, axis, plan):
        half, inward, outward, across, middle, lower = plan
        inverse, coupled, first, second = gains
        plane = last_gains.shape[1:]
        for hop in range(half - 1 if source is not None else 0):
            start = lax.ppermute(last, axis, inward)
            reduced, last = forward(source, gains, start, rows, lower)
        values = inner_values(last_gains, far_gains, last, axis, across)
        values = outer_values(values, rows, half, outward, middle, axis, lower, reduced, first, second)
        return reduced, values

    def forward(source, gains, start, rows, lower):
        inverse, coupled, first, second = gains
        return call(
            functools.partial(forward_body, rows),
            [field, shape(*start.shape)],
            [SMEM] + [VMEM] * 5,
            (lower, source, inverse, coupled, second, start),
        )

    plan_i = (half_i, in_i, out_i, across_i, middle_i, lower_i)
    plan_j = (half_j, in_j, out_j, across_j, middle_j, lower_j)
    source_i = None
    if half_i > 1:
        correction = jnp.zeros_like(reduced)
        base, base_last = reduced, last
        for hop in range(half_i - 1):
            start = lax.ppermute(last, "ia", in_i)
            correction, correction_last = forward(jnp.zeros_like(base), gains_i, start, rows_i, lower_i)
            last = base_last + correction_last
        reduced = base + correction
    reduced, values = sweep(None, reduced, last, gains_i, last_i, far_i, rows_i, "ia", plan_i)
    (turned,) = call(
        functools.partial(turn_body, rows_i),
        [field],
        [SMEM] + [VMEM] * 4,
        (lower_i, reduced, first, second, values),
    )

    reduced, last = forward(turned, gains_j, jnp.zeros((2,) + j_plane, F32), rows_j, lower_j)
    reduced, values = sweep(turned, reduced, last, gains_j, last_j, far_j, rows_j, "ja", plan_j)
    depth = -(-variables * (total // LANES) // BS) * BS
    inverse, coupled, first, second = gains_j
    advanced, increment = call(
        functools.partial(finish_body, rows_j),
        [field, field],
        [SMEM, SMEM, SMEM] + [VMEM] * 6,
        (lower_j, speeds, right, reduced, first, second, values, rho, filled),
        scratch=[pltpu.VMEM((variables, total, rows_k), F32)]
        + [pltpu.VMEM((rows_k * depth, LANES), F32)] * 4,
    )
    return advanced.reshape(flow_state.shape), increment.reshape(flow_state.shape)


def solution(mesh):
    return jax.shard_map(
        local,
        mesh=mesh,
        in_specs=(
            P(None, "ka", "ia", "ja", None),
            P(None, "ka", "ia", "ja", None),
            P(None, "ka", None),
            P("ka", None, None),
            P("ka", None, None),
            P(("ia", "ja", "ka"), None, None),
            P(("ia", "ja", "ka"), None, None),
            P(("ia", "ja", "ka"), None),
            P(None, ("ia", "ja", "ka"), None, None),
        ),
        out_specs=(P(None, "ka", "ia", "ja", None), P(None, "ka", "ia", "ja", None)),
        check_vma=False,
    )
```

```python
import functools
import math

import jax
import jax.numpy as jnp
from jax import lax
from jax.experimental import pallas as pl
from jax.experimental.pallas import tpu as pltpu
from jax.sharding import PartitionSpec as P

BS = 8
LANES = 128
GROUPS = LANES // BS
QUARTER = 0.25
VMEM = pl.BlockSpec(memory_space=pltpu.VMEM)
SMEM = pl.BlockSpec(memory_space=pltpu.SMEM)
F32 = jnp.float32


def call(body, outs, ins, args, scratch=(), flops=4_000_000, collective_id=None):
    moved = sum(a.size * 4 for a in args) + sum(o.size * 4 for o in outs)
    held = sum(math.prod(r.shape) * 4 for r in scratch if math.prod(r.shape) > 1024)
    options = {} if collective_id is None else {"collective_id": collective_id, "has_side_effects": True}
    return pl.pallas_call(
        body,
        out_shape=outs,
        in_specs=ins,
        out_specs=[VMEM] * len(outs),
        scratch_shapes=list(scratch),
        compiler_params=pltpu.CompilerParams(vmem_limit_bytes=moved + held + (3 << 20), **options),
        cost_estimate=pl.CostEstimate(flops=flops, bytes_accessed=moved, transcendentals=0),
    )(*args)


def shape(*dims):
    return jax.ShapeDtypeStruct(dims, F32)


def lane_iota():
    return lax.broadcasted_iota(jnp.int32, (BS, LANES), 1)


def split_block(block, blocks_j):
    along_k = block % GROUPS
    rest = block // GROUPS
    return rest // blocks_j, rest % blocks_j, along_k


def pack_body(rows_j, donor, flow, outbound):
    variables = flow.shape[0]
    group = lane_iota() // BS

    def one(slot, carry):
        block_i, block_j, block_k = split_block(donor[slot], rows_j // BS)
        first = block_i * (BS * rows_j) + block_j * BS
        tiles = [jnp.zeros((BS, LANES), F32) for q in range(outbound.shape[1] // BS)]
        for g in range(variables * BS):
            row = pl.multiple_of(first + (g % BS) * rows_j, BS)
            tile = flow[g // BS, pl.ds(row, BS), :]
            moved = pltpu.roll(tile, (g * BS - block_k * BS + 8 * LANES) % LANES, 1)
            tiles[g // GROUPS] = jnp.where(group == g % GROUPS, moved, tiles[g // GROUPS])
        for q, tile in enumerate(tiles):
            outbound[slot, q * BS : (q + 1) * BS, :] = tile
        return carry

    lax.fori_loop(0, outbound.shape[0], one, 0)


def blend(cubes, shifted, weight):
    return (1.0 - weight) * cubes + weight * shifted


def fill_body(rows_j, capacity, receiver, count, weights, flow, arrived, filled):
    variables = flow.shape[0]
    slots, packed_rows, lanes = arrived.shape
    group = lane_iota() // BS
    lane = lax.broadcasted_iota(jnp.int32, (packed_rows, LANES), 1)
    row = lax.broadcasted_iota(jnp.int32, (packed_rows, LANES), 0)
    filled[...] = flow[...]

    def one(slot, carry):
        @pl.when(slot % capacity < count[slot // capacity])
        def _():
            cubes = arrived[slot]
            after = jnp.where(lane % (BS * BS) >= BS * (BS - 1), cubes, pltpu.roll(cubes, LANES - BS, 1))
            cubes = blend(cubes, after, weights[slot])
            after = jnp.where(row % BS == BS - 1, cubes, pltpu.roll(cubes, packed_rows - 1, 0))
            cubes = blend(cubes, after, weights[slots + slot])
            after = jnp.where(lane % BS == BS - 1, cubes, pltpu.roll(cubes, LANES - 1, 1))
            cubes = blend(cubes, after, weights[2 * slots + slot])
            block_i, block_j, block_k = split_block(receiver[slot], rows_j // BS)
            first = block_i * (BS * rows_j) + block_j * BS
            here = group == block_k
            for g in range(variables * BS):
                q = g // GROUPS
                tile = cubes[q * BS : (q + 1) * BS]
                moved = pltpu.roll(tile, (block_k * BS - g * BS + 8 * LANES) % LANES, 1)
                at = pl.ds(pl.multiple_of(first + (g % BS) * rows_j, BS), BS)
                filled[g // BS, at, :] = jnp.where(here, moved, filled[g // BS, at, :])

        return carry

    lax.fori_loop(0, slots, one, 0)


def eliminate(coupling, older_first, older_second, last_first, last_second):
    fourth = QUARTER * coupling
    coupled = -coupling + fourth * older_first
    pivots = 1.0 + 2.5 * coupling + fourth * older_second - last_first * coupled
    inverse = 1.0 / pivots
    first = (-coupling - last_second * coupled) * inverse
    second = -fourth * inverse
    return inverse, coupled * inverse, first, second


def meet(gains, values, far_gains, far_values):
    f0, s0, f1, s1 = gains
    g0, t0, g1, t1 = far_gains
    r0, r1 = values
    q0, q1 = far_values
    cross = g1 - t1 * f0
    a11 = 1.0 - t1 * s0 - cross * f1
    a12 = -cross * s1
    b1 = q1 - t1 * r0 - cross * r1
    a21 = g0 - t0 * f1
    a22 = 1.0 - t0 * s1
    b2 = q0 - t0 * r1
    scale = 1.0 / (a11 * a22 - a12 * a21)
    return (b1 * a22 - a12 * b2) * scale, (a11 * b2 - a21 * b1) * scale


def row_of(n, count, lower):
    return jnp.where(lower, n, count - 1 - n)


def factor_pass(direction, rows, stride, is_lower, speeds, spectral, start, outs, last):
    inverse, coupled, first, second = outs
    variables, total, lanes = inverse.shape
    plane = total // rows

    def one(n, carry):
        row = row_of(n, rows, is_lower)
        at = pl.ds(pl.multiple_of(row * plane, BS), plane)
        if stride is None:
            rho = spectral[direction, at, :]
        else:
            rho = spectral[direction, pl.ds(row, plane, stride=stride), :]
        fresh = []
        for v in range(variables):
            older_first, older_second, last_first, last_second = carry[v]
            a, b, c, d = eliminate(
                speeds[direction * variables + v] * rho, older_first, older_second, last_first, last_second
            )
            inverse[v, at, :] = a
            coupled[v, at, :] = b
            first[v, at, :] = c
            second[v, at, :] = d
            fresh.append((last_first, last_second, c, d))
        return tuple(fresh)

    begin = tuple(tuple(start[m, v] for m in range(4)) for v in range(variables))
    ends = lax.fori_loop(0, rows, one, begin)
    for v in range(variables):
        for m in range(4):
            last[m, v] = ends[v][m]


class Line:
    def __init__(self, axis):
        self.axis = axis
        self.members = lax.axis_size(axis)
        self.half = self.members // 2
        self.place = lax.axis_index(axis)
        self.lower = self.place < self.half
        self.depth = jnp.where(self.lower, self.place, self.members - 1 - self.place)
        self.inner = jnp.where(self.lower, self.place + 1, self.place - 1)
        self.outer = jnp.where(self.lower, self.place - 1, self.place + 1)
        self.middle = self.depth == self.half - 1
        self.end = self.depth == 0

    def send(self, source, target, sems, device):
        return pltpu.make_async_remote_copy(
            src_ref=source,
            dst_ref=target,
            send_sem=sems.at[0],
            recv_sem=sems.at[1],
            device_id={self.axis: device},
            device_id_type=pl.DeviceIdType.MESH,
        )


def take_start(line, source, start, sems):
    @pl.when(line.end)
    def _():
        start[...] = jnp.zeros(start.shape, F32)

    if line.half > 1:

        @pl.when(jnp.logical_not(line.end))
        def _():
            line.send(source, start, sems, line.inner).wait_recv()


def send_inward(line, source, start, start_sems, far, far_sems):
    if line.half > 1:

        @pl.when(jnp.logical_not(line.middle))
        def _():
            line.send(source, start, start_sems, line.inner).start()

    @pl.when(line.middle)
    def _():
        line.send(source, far, far_sems, line.inner).start()


def end_inward(line, source, start, start_sems, far, far_sems):
    if line.half > 1:

        @pl.when(jnp.logical_not(line.middle))
        def _():
            line.send(source, start, start_sems, line.inner).wait_send()

    @pl.when(line.middle)
    def _():
        line.send(source, far, far_sems, line.inner).wait_send()


def peer_of(number, axes):
    rest, place = number, {}
    for axis in reversed(axes):
        place[axis] = rest % lax.axis_size(axis)
        rest = rest // lax.axis_size(axis)
    return place


def exchange_body(axes, capacity, rows_i, rows_j, speeds, outbound, spectral, arrived, *refs):
    gains_i, (last_i, far_i), gains_j, (last_j, far_j) = refs[:4], refs[4:6], refs[6:10], refs[10:12]
    start_i, start_j, sent, got, i_start, i_far, j_start, j_far = refs[12:]
    devices = 1
    me = 0
    for axis in axes:
        devices = devices * lax.axis_size(axis)
        me = me * lax.axis_size(axis) + lax.axis_index(axis)
    barrier = pltpu.get_barrier_semaphore()

    def greet(step, carry):
        peer = peer_of((me + step) % devices, axes)
        pl.semaphore_signal(barrier, inc=1, device_id=peer, device_id_type=pl.DeviceIdType.MESH)
        return carry

    lax.fori_loop(1, devices, greet, 0)
    pl.semaphore_wait(barrier, devices - 1)

    def slots(device):
        return pl.ds(device * capacity, capacity)

    def cubes(step, to, of):
        return pltpu.make_async_remote_copy(
            src_ref=outbound.at[slots(to)],
            dst_ref=arrived.at[slots(of)],
            send_sem=sent.at[step],
            recv_sem=got.at[step],
            device_id=peer_of(to, axes),
            device_id_type=pl.DeviceIdType.MESH,
        )

    def begin(step, carry):
        cubes(step, (me + step) % devices, me).start()
        return carry

    lax.fori_loop(1, devices, begin, 0)
    arrived[slots(me)] = outbound[slots(me)]

    line_i, line_j = Line("ia"), Line("ja")

    def eliminate_i():
        take_start(line_i, last_i, start_i, i_start)
        factor_pass(0, rows_i, None, line_i.lower, speeds, spectral, start_i, gains_i, last_i)
        send_inward(line_i, last_i, start_i, i_start, far_i, i_far)

    take_start(line_j, last_j, start_j, j_start)
    factor_pass(1, rows_j, rows_j, line_j.lower, speeds, spectral, start_j, gains_j, last_j)
    send_inward(line_j, last_j, start_j, j_start, far_j, j_far)
    eliminate_i()

    for line, last, far, far_sems, start, start_sems in (
        (line_i, last_i, far_i, i_far, start_i, i_start),
        (line_j, last_j, far_j, j_far, start_j, j_start),
    ):
        end_inward(line, last, start, start_sems, far, far_sems)

        @pl.when(line.middle)
        def _():
            line.send(last, far, far_sems, line.inner).wait_recv()

        @pl.when(jnp.logical_not(line.middle))
        def _():
            far[...] = jnp.zeros(far.shape, F32)

    def end(step, carry):
        of = (me + devices - step) % devices
        cubes(step, (me + step) % devices, of).wait_recv()
        cubes(step, (me + step) % devices, of).wait_send()
        return carry

    lax.fori_loop(1, devices, end, 0)


def residual_pass(
    rows_i, is_lower, left, padded, spectral, j_before, j_after, inverse, coupled, second, start, reduced, last
):
    variables, total, lanes = inverse.shape
    rows_j = total // rows_i
    lane = lax.broadcasted_iota(jnp.int32, (rows_j, lanes), 1)
    row_id = lax.broadcasted_iota(jnp.int32, (rows_j, lanes), 0)

    def one(n, carry):
        row = row_of(n, rows_i, is_lower)
        base = pl.multiple_of(row * rows_j, BS)
        at = pl.ds(base, rows_j)
        rho = [spectral[e, at, :] for e in range(3)]
        residual = []
        for v in range(variables):
            center = padded[v, pl.ds(base + rows_j, rows_j), :]
            twice = 2.0 * center
            along_i = padded[v, pl.ds(base + 2 * rows_j, rows_j), :] + padded[v, at, :] - twice
            after = jnp.where(
                row_id == rows_j - 1, j_after[v, pl.ds(row, 1), :], pltpu.roll(center, rows_j - 1, 0)
            )
            before = jnp.where(row_id == 0, j_before[v, pl.ds(row, 1), :], pltpu.roll(center, 1, 0))
            along_j = after + before - twice
            after = jnp.where(lane == lanes - 1, 0.0, pltpu.roll(center, lanes - 1, 1))
            before = jnp.where(lane == 0, 0.0, pltpu.roll(center, 1, 1))
            along_k = after + before - twice
            residual.append(rho[0] * along_i + rho[1] * along_j + rho[2] * along_k)
        fresh = []
        for v in range(variables):
            source = left[v * variables] * residual[0]
            for u in range(1, variables):
                source = source + left[v * variables + u] * residual[u]
            older, newer = carry[v]
            value = source * inverse[v, at, :] - second[v, at, :] * older - coupled[v, at, :] * newer
            reduced[v, at, :] = value
            fresh.append((newer, value))
        return tuple(fresh)

    ends = lax.fori_loop(0, rows_i, one, begin_of(start, variables))
    for v in range(variables):
        last[0, v] = ends[v][0]
        last[1, v] = ends[v][1]


def forward_pass(rows, is_lower, source, inverse, coupled, second, start, reduced, last):
    variables, total, lanes = source.shape
    plane = total // rows

    def one(n, carry):
        at = pl.ds(pl.multiple_of(row_of(n, rows, is_lower) * plane, BS), plane)
        fresh = []
        for v in range(variables):
            older, newer = carry[v]
            value = (
                source[v, at, :] * inverse[v, at, :]
                - second[v, at, :] * older
                - coupled[v, at, :] * newer
            )
            reduced[v, at, :] = value
            fresh.append((newer, value))
        return tuple(fresh)

    begin = tuple((start[0, v], start[1, v]) for v in range(variables))
    ends = lax.fori_loop(0, rows, one, begin)
    for v in range(variables):
        last[0, v] = ends[v][0]
        last[1, v] = ends[v][1]


def backward_pass(rows, is_lower, reduced, first, second, begin, store):
    variables, total, lanes = reduced.shape
    plane = total // rows

    def one(step, carry):
        row = row_of(rows - 1 - step, rows, is_lower)
        at = pl.ds(pl.multiple_of(row * plane, BS), plane)
        fresh = []
        for v in range(variables):
            nearer, farther = carry[v]
            value = reduced[v, at, :] - first[v, at, :] * nearer - second[v, at, :] * farther
            store(v, row, value)
            fresh.append((value, nearer))
        return tuple(fresh)

    return lax.fori_loop(0, rows, one, begin)


def start_values(variables, gains, values, far_gains, far_values):
    return tuple(
        meet(
            [gains[m, v] for m in range(4)],
            [values[m, v] for m in range(2)],
            [far_gains[m, v] for m in range(4)],
            [far_values[m, v] for m in range(2)],
        )
        for v in range(variables)
    )


def begin_of(next_values, variables):
    return tuple((next_values[0, v], next_values[1, v]) for v in range(variables))


def solve_back(line, rows, reduced, gains, last_gains, far_gains, last, far, far_sems, nexts, next_sems, solved, store):
    variables = reduced.shape[0]

    @pl.when(line.middle)
    def _():
        line.send(last, far, far_sems, line.inner).wait_recv()
        for v, pair in enumerate(start_values(variables, last_gains, last, far_gains, far)):
            nexts[0, v] = pair[0]
            nexts[1, v] = pair[1]

    if line.half > 1:

        @pl.when(jnp.logical_not(line.middle))
        def _():
            line.send(solved, nexts, next_sems, line.outer).wait_recv()

    ends = backward_pass(
        rows, line.lower, reduced, gains[2], gains[3], begin_of(nexts, variables), store
    )
    if line.half > 1:
        for v in range(variables):
            solved[0, v] = ends[v][0]
            solved[1, v] = ends[v][1]

        @pl.when(jnp.logical_not(line.end))
        def _():
            line.send(solved, nexts, next_sems, line.outer).start()


def sweep_body(rows_i, rows_j, left, filled, spectral, *refs):
    gains_i, (last_gains_i, far_gains_i) = refs[:4], refs[4:6]
    gains_j, (last_gains_j, far_gains_j) = refs[6:10], refs[10:12]
    lines = refs[12]
    (padded, reduced, turned, i_halo, j_edge, j_halo, halo_sems) = refs[13:20]
    ends_i, start_i, far_i, nexts_i, solved_i, sems_i = refs[20:26]
    ends_j, start_j, far_j, nexts_j, solved_j, sems_j = refs[26:32]
    variables, total, lanes = filled.shape
    line_i, line_j = Line("ia"), Line("ja")
    barrier = pltpu.get_barrier_semaphore()

    def sides(line):
        return (line.place > 0, line.place - 1), (line.place < line.members - 1, line.place + 1)

    heard = 0
    for line in (line_i, line_j):
        for there, device in sides(line):
            heard = heard + there.astype(jnp.int32)

            @pl.when(there)
            def _():
                pl.semaphore_signal(
                    barrier, inc=1, device_id={line.axis: device}, device_id_type=pl.DeviceIdType.MESH
                )

    for v in range(variables):
        j_edge[0, v] = filled[v, pl.ds(0, rows_i, stride=rows_j), :]
        j_edge[1, v] = filled[v, pl.ds(rows_j - 1, rows_i, stride=rows_j), :]
    pl.semaphore_wait(barrier, heard)

    def edges(axis_number, side):
        if axis_number == 1:
            return j_edge.at[side], j_halo.at[1 - side]
        first = 0 if side == 0 else total - rows_j
        return filled.at[:, pl.ds(first, rows_j), :], i_halo.at[1 - side]

    def halo(line, axis_number, side, device):
        source, target = edges(axis_number, side)
        number = axis_number * 2 + side
        return pltpu.make_async_remote_copy(
            src_ref=source,
            dst_ref=target,
            send_sem=halo_sems.at[0, number],
            recv_sem=halo_sems.at[1, number],
            device_id={line.axis: device},
            device_id_type=pl.DeviceIdType.MESH,
        )

    for axis_number, line in ((1, line_j), (0, line_i)):
        for side, (there, device) in enumerate(sides(line)):

            @pl.when(there)
            def _():
                halo(line, axis_number, side, device).start()

    padded[:, rows_j : rows_j + total, :] = filled[...]
    for axis_number, line in ((0, line_i), (1, line_j)):
        for side, (there, device) in enumerate(sides(line)):
            target = (i_halo, j_halo)[axis_number]

            @pl.when(there)
            def _():
                halo(line, axis_number, 1 - side, device).wait_recv()

            @pl.when(jnp.logical_not(there))
            def _():
                target[side] = jnp.zeros(target.shape[1:], F32)

    padded[:, :rows_j, :] = i_halo[0]
    padded[:, rows_j + total :, :] = i_halo[1]

    take_start(line_i, ends_i, start_i, sems_i.at[0])
    residual_pass(
        rows_i, line_i.lower, left, padded, spectral, j_halo.at[0], j_halo.at[1],
        gains_i[0], gains_i[1], gains_i[3], start_i, reduced, ends_i,
    )
    send_inward(line_i, ends_i, start_i, sems_i.at[0], far_i, sems_i.at[1])

    def store_turned(v, row, value):
        turned[v, pl.ds(row, rows_j, stride=rows_i), :] = value

    solve_back(
        line_i, rows_i, reduced, gains_i, last_gains_i, far_gains_i, ends_i, far_i, sems_i.at[1],
        nexts_i, sems_i.at[2], solved_i, store_turned,
    )

    take_start(line_j, ends_j, start_j, sems_j.at[0])
    forward_pass(
        rows_j, line_j.lower, turned, gains_j[0], gains_j[1], gains_j[3], start_j, reduced, ends_j
    )
    send_inward(line_j, ends_j, start_j, sems_j.at[0], far_j, sems_j.at[1])

    def store_lines(v, row, value):
        lines[v, pl.ds(pl.multiple_of(row * rows_i, BS), rows_i), :] = value

    solve_back(
        line_j, rows_j, reduced, gains_j, last_gains_j, far_gains_j, ends_j, far_j, sems_j.at[1],
        nexts_j, sems_j.at[2], solved_j, store_lines,
    )

    for axis_number, line in ((0, line_i), (1, line_j)):
        for side, (there, device) in enumerate(sides(line)):

            @pl.when(there)
            def _():
                halo(line, axis_number, side, device).wait_send()

    for line, ends, start, far, nexts, solved, sems in (
        (line_i, ends_i, start_i, far_i, nexts_i, solved_i, sems_i),
        (line_j, ends_j, start_j, far_j, nexts_j, solved_j, sems_j),
    ):
        end_inward(line, ends, start, sems.at[0], far, sems.at[1])
        if line.half > 1:

            @pl.when(jnp.logical_not(line.end))
            def _():
                line.send(solved, nexts, sems.at[2], line.outer).wait_send()


def finish_body(
    rows_j, speeds, right, lines, spectral, filled,
    advanced, increment, values, coupling, gain_1, gain_2,
):
    variables, total, lanes = lines.shape
    rows_i = total // rows_j
    quarters = total // LANES
    per_quarter = LANES // rows_i
    depth = values.shape[0] // lanes

    for q in range(quarters):
        rho = jnp.concatenate(
            [
                spectral[2, pl.ds(q * per_quarter + j, rows_i, stride=rows_j), :]
                for j in range(per_quarter)
            ],
            axis=0,
        ).T
        for v in range(variables):
            at = pl.ds(v * quarters + q, lanes, stride=depth)
            coupling[at, :] = speeds[2 * variables + v] * rho
            values[at, :] = lines[v, q * LANES : (q + 1) * LANES, :].T
    for spare in range(variables * quarters, depth):
        at = pl.ds(spare, lanes, stride=depth)
        coupling[at, :] = jnp.zeros((lanes, lanes), F32)
        values[at, :] = jnp.zeros((lanes, lanes), F32)

    half = lanes // 2
    gain_1[:depth, :] = jnp.zeros((depth, lanes), F32)
    zero = gain_1[:depth, :]

    def ahead(n, carry):
        fresh = []
        for side in range(2):
            older_first, older_second, older, last_first, last_second, newer = carry[side]
            k = n if side == 0 else lanes - 1 - n
            at = pl.ds(pl.multiple_of(k * depth, BS), depth)
            inverse, coupled, one, two = eliminate(
                coupling[at, :], older_first, older_second, last_first, last_second
            )
            value = values[at, :] * inverse - two * older - coupled * newer
            gain_1[at, :] = one
            gain_2[at, :] = two
            values[at, :] = value
            fresh.append((last_first, last_second, newer, one, two, value))
        return tuple(fresh)

    low, high = lax.fori_loop(0, half, ahead, ((zero,) * 6,) * 2)

    def ends(side):
        return [side[0], side[1], side[3], side[4]], [side[2], side[5]]

    low_next = meet(*ends(low), *ends(high))
    high_next = meet(*ends(high), *ends(low))

    def back(step, carry):
        fresh = []
        for side in range(2):
            nearer, farther = carry[side]
            n = half - 1 - step
            k = n if side == 0 else lanes - 1 - n
            at = pl.ds(pl.multiple_of(k * depth, BS), depth)
            value = values[at, :] - gain_1[at, :] * nearer - gain_2[at, :] * farther
            values[at, :] = value
            fresh.append((value, nearer))
        return tuple(fresh)

    lax.fori_loop(0, half, back, (low_next, high_next))
    for q in range(quarters):
        solved = [values[pl.ds(u * quarters + q, lanes, stride=depth), :] for u in range(variables)]
        for v in range(variables):
            total_v = right[v * variables] * solved[0]
            for u in range(1, variables):
                total_v = total_v + right[v * variables + u] * solved[u]
            turned = total_v.T
            for j in range(per_quarter):
                at = pl.ds(q * per_quarter + j, rows_i, stride=rows_j)
                piece = turned[j * rows_i : (j + 1) * rows_i]
                increment[v, at, :] = piece
                advanced[v, at, :] = filled[v, at, :] + piece


def local(
    flow_state, spectral, wave_speed, left_map, right_map,
    donor_block, receiver_block, fringe_count, fringe_weight,
):
    variables, grids, rows_i, rows_j, rows_k = flow_state.shape
    assert grids == 1 and rows_k == LANES
    total = rows_i * rows_j
    devices, capacity = donor_block.shape[1:]
    slots = devices * capacity
    flow = flow_state.reshape(variables, total, rows_k)
    rho = spectral.reshape(3, total, rows_k)
    speeds = wave_speed.reshape(-1)
    left = left_map.reshape(-1)
    right = right_map.reshape(-1)
    packed_rows = -(-variables * BS // GROUPS) * BS
    field = shape(variables, total, rows_k)
    i_plane = (variables, rows_j, rows_k)
    j_plane = (variables, rows_i, rows_k)
    axes = ("ia", "ja", "ka")

    (outbound,) = call(
        functools.partial(pack_body, rows_j),
        [shape(slots, packed_rows, LANES)],
        [SMEM, VMEM],
        (donor_block.reshape(-1), flow),
    )
    dma = pltpu.SemaphoreType.DMA
    arrived, *gains = call(
        functools.partial(exchange_body, axes, capacity, rows_i, rows_j),
        [shape(slots, packed_rows, LANES)]
        + [field] * 4
        + [shape(4, *i_plane)] * 2
        + [field] * 4
        + [shape(4, *j_plane)] * 2,
        [SMEM, VMEM, VMEM],
        (speeds, outbound, rho),
        scratch=[pltpu.VMEM((4,) + i_plane, F32), pltpu.VMEM((4,) + j_plane, F32)]
        + [dma((devices,))] * 2
        + [dma((2,))] * 4,
        collective_id=0,
    )
    (filled,) = call(
        functools.partial(fill_body, rows_j, capacity),
        [field],
        [SMEM, SMEM, SMEM, VMEM, VMEM],
        (receiver_block.reshape(-1), fringe_count.reshape(-1), fringe_weight.reshape(-1), flow, arrived),
    )
    (lines,) = call(
        functools.partial(sweep_body, rows_i, rows_j),
        [field],
        [SMEM] + [VMEM] * 14,
        (left, filled, rho, *gains),
        scratch=[
            pltpu.VMEM((variables, total + 2 * rows_j, rows_k), F32),
            pltpu.VMEM((variables, total, rows_k), F32),
            pltpu.VMEM((variables, total, rows_k), F32),
            pltpu.VMEM((2,) + i_plane, F32),
            pltpu.VMEM((2,) + j_plane, F32),
            pltpu.VMEM((2,) + j_plane, F32),
            dma((2, 4)),
        ]
        + [pltpu.VMEM((2,) + i_plane, F32)] * 5
        + [dma((3, 2))]
        + [pltpu.VMEM((2,) + j_plane, F32)] * 5
        + [dma((3, 2))],
        collective_id=1,
    )
    depth = -(-variables * (total // LANES) // BS) * BS
    advanced, increment = call(
        functools.partial(finish_body, rows_j),
        [field, field],
        [SMEM, SMEM] + [VMEM] * 3,
        (speeds, right, lines, rho, filled),
        scratch=[pltpu.VMEM((rows_k * depth, LANES), F32)] * 4,
    )
    return advanced.reshape(flow_state.shape), increment.reshape(flow_state.shape)


def solution(mesh):
    return jax.shard_map(
        local,
        mesh=mesh,
        in_specs=(
            P(None, "ka", "ia", "ja", None),
            P(None, "ka", "ia", "ja", None),
            P(None, "ka", None),
            P("ka", None, None),
            P("ka", None, None),
            P(("ia", "ja", "ka"), None, None),
            P(("ia", "ja", "ka"), None, None),
            P(("ia", "ja", "ka"), None),
            P(None, ("ia", "ja", "ka"), None, None),
        ),
        out_specs=(P(None, "ka", "ia", "ja", None), P(None, "ka", "ia", "ja", None)),
        check_vma=False,
    )
```

```python
import functools
import math

import jax
import jax.numpy as jnp
from jax import lax
from jax.experimental import pallas as pl
from jax.experimental.pallas import tpu as pltpu
from jax.sharding import PartitionSpec as P

BS = 8
LANES = 128
GROUPS = LANES // BS
QUARTER = 0.25
VMEM = pl.BlockSpec(memory_space=pltpu.VMEM)
SMEM = pl.BlockSpec(memory_space=pltpu.SMEM)
F32 = jnp.float32


def call(body, outs, ins, args, scratch=(), flops=4_000_000, collective_id=None):
    moved = sum(a.size * 4 for a in args) + sum(o.size * 4 for o in outs)
    held = sum(math.prod(r.shape) * 4 for r in scratch if math.prod(r.shape) > 1024)
    options = {} if collective_id is None else {"collective_id": collective_id, "has_side_effects": True}
    return pl.pallas_call(
        body,
        out_shape=outs,
        in_specs=ins,
        out_specs=[VMEM] * len(outs),
        scratch_shapes=list(scratch),
        compiler_params=pltpu.CompilerParams(vmem_limit_bytes=moved + held + (3 << 20), **options),
        cost_estimate=pl.CostEstimate(flops=flops, bytes_accessed=moved, transcendentals=0),
    )(*args)


def shape(*dims):
    return jax.ShapeDtypeStruct(dims, F32)


def lane_iota():
    return lax.broadcasted_iota(jnp.int32, (BS, LANES), 1)


def groups_turned(tiles):
    group = lane_iota() // BS
    tiles = list(tiles)
    distance = 1
    while distance < GROUPS:
        upper = (group // distance) % 2 == 1
        shift = distance * BS
        for a in range(GROUPS):
            if a & distance == 0:
                x, y = tiles[a], tiles[a + distance]
                tiles[a] = jnp.where(upper, pltpu.roll(y, shift, 1), x)
                tiles[a + distance] = jnp.where(upper, y, pltpu.roll(x, LANES - shift, 1))
        distance *= 2
    return tiles


def tile_at(block, rows_j, g):
    blocks_j = rows_j // BS
    row = (block // blocks_j) * (BS * rows_j) + (block % blocks_j) * BS + (g % BS) * rows_j
    return pl.ds(pl.multiple_of(row, BS), BS)


def pack_all(rows_j, flow, packed):
    groups = flow.shape[0] * BS

    def one(block, carry):
        for first in range(0, groups, GROUPS):
            count = min(GROUPS, groups - first)
            tiles = [flow[g // BS, tile_at(block, rows_j, g), :] for g in range(first, first + count)]
            tiles = groups_turned(tiles + tiles[:1] * (GROUPS - count))
            q = first // GROUPS
            for k in range(GROUPS):
                packed[block * GROUPS + k, q * BS : (q + 1) * BS, :] = tiles[k]
        return carry

    lax.fori_loop(0, packed.shape[0] // GROUPS, one, 0)


def unpack_all(rows_j, source, packed, arrived, filled):
    groups = filled.shape[0] * BS

    def one(block, carry):
        for first in range(0, groups, GROUPS):
            q = first // GROUPS
            tiles = []
            for k in range(GROUPS):
                slot = source[block * GROUPS + k]
                live = jnp.full((BS, LANES), slot, jnp.int32) >= 0
                fresh = arrived[jnp.maximum(slot, 0), q * BS : (q + 1) * BS, :]
                kept = packed[block * GROUPS + k, q * BS : (q + 1) * BS, :]
                tiles.append(jnp.where(live, fresh, kept))
            tiles = groups_turned(tiles)
            for g in range(first, min(first + GROUPS, groups)):
                filled[g // BS, tile_at(block, rows_j, g), :] = tiles[g - first]
        return carry

    lax.fori_loop(0, packed.shape[0] // GROUPS, one, 0)


def blend(cubes, shifted, weight):
    return (1.0 - weight) * cubes + weight * shifted


def interpolate_all(weights, arrived):
    slots, packed_rows, lanes = arrived.shape
    lane = lax.broadcasted_iota(jnp.int32, (packed_rows, LANES), 1)
    row = lax.broadcasted_iota(jnp.int32, (packed_rows, LANES), 0)

    def one(slot, carry):
        cubes = arrived[slot]
        after = jnp.where(lane % (BS * BS) >= BS * (BS - 1), cubes, pltpu.roll(cubes, LANES - BS, 1))
        cubes = blend(cubes, after, weights[slot])
        after = jnp.where(row % BS == BS - 1, cubes, pltpu.roll(cubes, packed_rows - 1, 0))
        cubes = blend(cubes, after, weights[slots + slot])
        after = jnp.where(lane % BS == BS - 1, cubes, pltpu.roll(cubes, LANES - 1, 1))
        arrived[slot] = blend(cubes, after, weights[2 * slots + slot])
        return carry

    lax.fori_loop(0, slots, one, 0, unroll=4)


def eliminate(coupling, older_first, older_second, last_first, last_second):
    fourth = QUARTER * coupling
    coupled = -coupling + fourth * older_first
    pivots = 1.0 + 2.5 * coupling + fourth * older_second - last_first * coupled
    inverse = 1.0 / pivots
    first = (-coupling - last_second * coupled) * inverse
    second = -fourth * inverse
    return inverse, coupled * inverse, first, second


def meet(gains, values, far_gains, far_values):
    f0, s0, f1, s1 = gains
    g0, t0, g1, t1 = far_gains
    r0, r1 = values
    q0, q1 = far_values
    cross = g1 - t1 * f0
    a11 = 1.0 - t1 * s0 - cross * f1
    a12 = -cross * s1
    b1 = q1 - t1 * r0 - cross * r1
    a21 = g0 - t0 * f1
    a22 = 1.0 - t0 * s1
    b2 = q0 - t0 * r1
    scale = 1.0 / (a11 * a22 - a12 * a21)
    return (b1 * a22 - a12 * b2) * scale, (a11 * b2 - a21 * b1) * scale


def row_of(n, count, lower):
    return jnp.where(lower, n, count - 1 - n)


def factor_pass(direction, rows, stride, is_lower, speeds, spectral, start, outs, last):
    inverse, coupled, first, second = outs
    variables, total, lanes = inverse.shape
    plane = total // rows

    def one(n, carry):
        row = row_of(n, rows, is_lower)
        at = pl.ds(pl.multiple_of(row * plane, BS), plane)
        if stride is None:
            rho = spectral[direction, at, :]
        else:
            rho = spectral[direction, pl.ds(row, plane, stride=stride), :]
        fresh = []
        for v in range(variables):
            older_first, older_second, last_first, last_second = carry[v]
            a, b, c, d = eliminate(
                speeds[direction * variables + v] * rho, older_first, older_second, last_first, last_second
            )
            inverse[v, at, :] = a
            coupled[v, at, :] = b
            first[v, at, :] = c
            second[v, at, :] = d
            fresh.append((last_first, last_second, c, d))
        return tuple(fresh)

    begin = tuple(tuple(start[m, v] for m in range(4)) for v in range(variables))
    ends = lax.fori_loop(0, rows, one, begin)
    for v in range(variables):
        for m in range(4):
            last[m, v] = ends[v][m]


class Line:
    def __init__(self, axis):
        self.axis = axis
        self.members = lax.axis_size(axis)
        self.half = self.members // 2
        self.place = lax.axis_index(axis)
        self.lower = self.place < self.half
        self.depth = jnp.where(self.lower, self.place, self.members - 1 - self.place)
        self.inner = jnp.where(self.lower, self.place + 1, self.place - 1)
        self.outer = jnp.where(self.lower, self.place - 1, self.place + 1)
        self.middle = self.depth == self.half - 1
        self.end = self.depth == 0

    def send(self, source, target, sems, device):
        return pltpu.make_async_remote_copy(
            src_ref=source,
            dst_ref=target,
            send_sem=sems.at[0],
            recv_sem=sems.at[1],
            device_id={self.axis: device},
            device_id_type=pl.DeviceIdType.MESH,
        )


def take_start(line, source, start, sems):
    @pl.when(line.end)
    def _():
        start[...] = jnp.zeros(start.shape, F32)

    if line.half > 1:

        @pl.when(jnp.logical_not(line.end))
        def _():
            line.send(source, start, sems, line.inner).wait_recv()


def send_inward(line, source, start, start_sems, far, far_sems):
    if line.half > 1:

        @pl.when(jnp.logical_not(line.middle))
        def _():
            line.send(source, start, start_sems, line.inner).start()

    @pl.when(line.middle)
    def _():
        line.send(source, far, far_sems, line.inner).start()


def end_inward(line, source, start, start_sems, far, far_sems):
    if line.half > 1:

        @pl.when(jnp.logical_not(line.middle))
        def _():
            line.send(source, start, start_sems, line.inner).wait_send()

    @pl.when(line.middle)
    def _():
        line.send(source, far, far_sems, line.inner).wait_send()


def peer_of(number, axes):
    rest, place = number, {}
    for axis in reversed(axes):
        place[axis] = rest % lax.axis_size(axis)
        rest = rest // lax.axis_size(axis)
    return place


def residual_pass(
    rows_i, is_lower, left, padded, spectral, j_before, j_after, inverse, coupled, second, start, reduced, last
):
    variables, total, lanes = inverse.shape
    rows_j = total // rows_i
    lane = lax.broadcasted_iota(jnp.int32, (rows_j, lanes), 1)
    row_id = lax.broadcasted_iota(jnp.int32, (rows_j, lanes), 0)

    def one(n, carry):
        row = row_of(n, rows_i, is_lower)
        base = pl.multiple_of(row * rows_j, BS)
        at = pl.ds(base, rows_j)
        rho = [spectral[e, at, :] for e in range(3)]
        residual = []
        for v in range(variables):
            center = padded[v, pl.ds(base + rows_j, rows_j), :]
            twice = 2.0 * center
            along_i = padded[v, pl.ds(base + 2 * rows_j, rows_j), :] + padded[v, at, :] - twice
            after = jnp.where(
                row_id == rows_j - 1, j_after[v, pl.ds(row, 1), :], pltpu.roll(center, rows_j - 1, 0)
            )
            before = jnp.where(row_id == 0, j_before[v, pl.ds(row, 1), :], pltpu.roll(center, 1, 0))
            along_j = after + before - twice
            after = jnp.where(lane == lanes - 1, 0.0, pltpu.roll(center, lanes - 1, 1))
            before = jnp.where(lane == 0, 0.0, pltpu.roll(center, 1, 1))
            along_k = after + before - twice
            residual.append(rho[0] * along_i + rho[1] * along_j + rho[2] * along_k)
        fresh = []
        for v in range(variables):
            source = left[v * variables] * residual[0]
            for u in range(1, variables):
                source = source + left[v * variables + u] * residual[u]
            older, newer = carry[v]
            value = source * inverse[v, at, :] - second[v, at, :] * older - coupled[v, at, :] * newer
            reduced[v, at, :] = value
            fresh.append((newer, value))
        return tuple(fresh)

    ends = lax.fori_loop(0, rows_i, one, begin_of(start, variables))
    for v in range(variables):
        last[0, v] = ends[v][0]
        last[1, v] = ends[v][1]


def forward_pass(rows, is_lower, source, inverse, coupled, second, start, reduced, last):
    variables, total, lanes = source.shape
    plane = total // rows

    def one(n, carry):
        at = pl.ds(pl.multiple_of(row_of(n, rows, is_lower) * plane, BS), plane)
        fresh = []
        for v in range(variables):
            older, newer = carry[v]
            value = (
                source[v, at, :] * inverse[v, at, :]
                - second[v, at, :] * older
                - coupled[v, at, :] * newer
            )
            reduced[v, at, :] = value
            fresh.append((newer, value))
        return tuple(fresh)

    begin = tuple((start[0, v], start[1, v]) for v in range(variables))
    ends = lax.fori_loop(0, rows, one, begin)
    for v in range(variables):
        last[0, v] = ends[v][0]
        last[1, v] = ends[v][1]


def backward_pass(rows, is_lower, reduced, first, second, begin, store):
    variables, total, lanes = reduced.shape
    plane = total // rows

    def one(step, carry):
        row = row_of(rows - 1 - step, rows, is_lower)
        at = pl.ds(pl.multiple_of(row * plane, BS), plane)
        fresh = []
        for v in range(variables):
            nearer, farther = carry[v]
            value = reduced[v, at, :] - first[v, at, :] * nearer - second[v, at, :] * farther
            store(v, row, value)
            fresh.append((value, nearer))
        return tuple(fresh)

    return lax.fori_loop(0, rows, one, begin)


def start_values(variables, gains, values, far_gains, far_values):
    return tuple(
        meet(
            [gains[m, v] for m in range(4)],
            [values[m, v] for m in range(2)],
            [far_gains[m, v] for m in range(4)],
            [far_values[m, v] for m in range(2)],
        )
        for v in range(variables)
    )


def begin_of(next_values, variables):
    return tuple((next_values[0, v], next_values[1, v]) for v in range(variables))


def solve_back(line, rows, reduced, gains, last_gains, far_gains, last, far, far_sems, nexts, next_sems, solved, store):
    variables = reduced.shape[0]

    @pl.when(line.middle)
    def _():
        line.send(last, far, far_sems, line.inner).wait_recv()
        for v, pair in enumerate(start_values(variables, last_gains, last, far_gains, far)):
            nexts[0, v] = pair[0]
            nexts[1, v] = pair[1]

    if line.half > 1:

        @pl.when(jnp.logical_not(line.middle))
        def _():
            line.send(solved, nexts, next_sems, line.outer).wait_recv()

    ends = backward_pass(
        rows, line.lower, reduced, gains[2], gains[3], begin_of(nexts, variables), store
    )
    if line.half > 1:
        for v in range(variables):
            solved[0, v] = ends[v][0]
            solved[1, v] = ends[v][1]

        @pl.when(jnp.logical_not(line.end))
        def _():
            line.send(solved, nexts, next_sems, line.outer).start()


def step_body(
    axes, capacity, rows_i, rows_j, speeds, left, right, donor, source, weights, flow, spectral,
    advanced, increment, *refs,
):
    packed, outbound, arrived, filled = refs[:4]
    gains_i, (last_gains_i, far_gains_i, start_gains_i) = refs[4:8], refs[8:11]
    gains_j, (last_gains_j, far_gains_j, start_gains_j) = refs[11:15], refs[15:18]
    sent, got, gain_sems_i, gain_sems_j = refs[18:22]
    (padded, reduced, turned, i_halo, j_edge, j_halo, halo_sems) = refs[22:29]
    ends_i, start_i, far_i, nexts_i, solved_i, sems_i = refs[29:35]
    ends_j, start_j, far_j, nexts_j, solved_j, sems_j = refs[35:41]
    lines, thirds = refs[41], refs[42:]
    variables, total, lanes = flow.shape
    line_i, line_j = Line("ia"), Line("ja")
    devices = 1
    me = 0
    for axis in axes:
        devices = devices * lax.axis_size(axis)
        me = me * lax.axis_size(axis) + lax.axis_index(axis)
    barrier = pltpu.get_barrier_semaphore()

    def greet(step, carry):
        peer = peer_of((me + step) % devices, axes)
        pl.semaphore_signal(barrier, inc=1, device_id=peer, device_id_type=pl.DeviceIdType.MESH)
        return carry

    lax.fori_loop(1, devices, greet, 0)
    pack_all(rows_j, flow, packed)

    def gather(slot, carry):
        outbound[slot] = packed[donor[slot]]
        return carry

    lax.fori_loop(0, devices * capacity, gather, 0, unroll=4)
    pl.semaphore_wait(barrier, devices - 1)

    def slots(device):
        return pl.ds(device * capacity, capacity)

    def cubes(step, to, of):
        return pltpu.make_async_remote_copy(
            src_ref=outbound.at[slots(to)],
            dst_ref=arrived.at[slots(of)],
            send_sem=sent.at[step],
            recv_sem=got.at[step],
            device_id=peer_of(to, axes),
            device_id_type=pl.DeviceIdType.MESH,
        )

    def begin(step, carry):
        cubes(step, (me + step) % devices, me).start()
        return carry

    lax.fori_loop(1, devices, begin, 0)
    arrived[slots(me)] = outbound[slots(me)]

    for direction, line, rows, stride, gains, last, far, start, sems in (
        (1, line_j, rows_j, rows_j, gains_j, last_gains_j, far_gains_j, start_gains_j, gain_sems_j),
        (0, line_i, rows_i, None, gains_i, last_gains_i, far_gains_i, start_gains_i, gain_sems_i),
    ):
        take_start(line, last, start, sems.at[0])
        factor_pass(direction, rows, stride, line.lower, speeds, spectral, start, gains, last)
        send_inward(line, last, start, sems.at[0], far, sems.at[1])

    def end(step, carry):
        cubes(step, (me + step) % devices, (me + devices - step) % devices).wait_recv()
        return carry

    lax.fori_loop(1, devices, end, 0)
    interpolate_all(weights, arrived)
    unpack_all(rows_j, source, packed, arrived, filled)

    def sides(line):
        return (line.place > 0, line.place - 1), (line.place < line.members - 1, line.place + 1)

    for v in range(variables):
        j_edge[0, v] = filled[v, pl.ds(0, rows_i, stride=rows_j), :]
        j_edge[1, v] = filled[v, pl.ds(rows_j - 1, rows_i, stride=rows_j), :]
    def edges(axis_number, side):
        if axis_number == 1:
            return j_edge.at[side], j_halo.at[1 - side]
        first = 0 if side == 0 else total - rows_j
        return filled.at[:, pl.ds(first, rows_j), :], i_halo.at[1 - side]

    def halo(line, axis_number, side, device):
        source, target = edges(axis_number, side)
        number = axis_number * 2 + side
        return pltpu.make_async_remote_copy(
            src_ref=source,
            dst_ref=target,
            send_sem=halo_sems.at[0, number],
            recv_sem=halo_sems.at[1, number],
            device_id={line.axis: device},
            device_id_type=pl.DeviceIdType.MESH,
        )

    for axis_number, line in ((1, line_j), (0, line_i)):
        for side, (there, device) in enumerate(sides(line)):

            @pl.when(there)
            def _():
                halo(line, axis_number, side, device).start()

    padded[:, rows_j : rows_j + total, :] = filled[...]
    for axis_number, line in ((0, line_i), (1, line_j)):
        for side, (there, device) in enumerate(sides(line)):
            target = (i_halo, j_halo)[axis_number]

            @pl.when(there)
            def _():
                halo(line, axis_number, 1 - side, device).wait_recv()

            @pl.when(jnp.logical_not(there))
            def _():
                target[side] = jnp.zeros(target.shape[1:], F32)

    padded[:, :rows_j, :] = i_halo[0]
    padded[:, rows_j + total :, :] = i_halo[1]

    take_start(line_i, ends_i, start_i, sems_i.at[0])
    residual_pass(
        rows_i, line_i.lower, left, padded, spectral, j_halo.at[0], j_halo.at[1],
        gains_i[0], gains_i[1], gains_i[3], start_i, reduced, ends_i,
    )
    send_inward(line_i, ends_i, start_i, sems_i.at[0], far_i, sems_i.at[1])

    def store_turned(v, row, value):
        turned[v, pl.ds(row, rows_j, stride=rows_i), :] = value

    @pl.when(line_i.middle)
    def _():
        line_i.send(last_gains_i, far_gains_i, gain_sems_i.at[1], line_i.inner).wait_recv()

    solve_back(
        line_i, rows_i, reduced, gains_i, last_gains_i, far_gains_i, ends_i, far_i, sems_i.at[1],
        nexts_i, sems_i.at[2], solved_i, store_turned,
    )

    take_start(line_j, ends_j, start_j, sems_j.at[0])
    forward_pass(
        rows_j, line_j.lower, turned, gains_j[0], gains_j[1], gains_j[3], start_j, reduced, ends_j
    )
    send_inward(line_j, ends_j, start_j, sems_j.at[0], far_j, sems_j.at[1])

    def store_lines(v, row, value):
        lines[v, pl.ds(pl.multiple_of(row * rows_i, BS), rows_i), :] = value

    @pl.when(line_j.middle)
    def _():
        line_j.send(last_gains_j, far_gains_j, gain_sems_j.at[1], line_j.inner).wait_recv()

    solve_back(
        line_j, rows_j, reduced, gains_j, last_gains_j, far_gains_j, ends_j, far_j, sems_j.at[1],
        nexts_j, sems_j.at[2], solved_j, store_lines,
    )

    for axis_number, line in ((0, line_i), (1, line_j)):
        for side, (there, device) in enumerate(sides(line)):

            @pl.when(there)
            def _():
                halo(line, axis_number, side, device).wait_send()

    def close(step, carry):
        cubes(step, (me + step) % devices, me).wait_send()
        return carry

    lax.fori_loop(1, devices, close, 0)
    end_inward(line_i, last_gains_i, start_gains_i, gain_sems_i.at[0], far_gains_i, gain_sems_i.at[1])
    end_inward(line_j, last_gains_j, start_gains_j, gain_sems_j.at[0], far_gains_j, gain_sems_j.at[1])
    for line, ends, start, far, nexts, solved, sems in (
        (line_i, ends_i, start_i, far_i, nexts_i, solved_i, sems_i),
        (line_j, ends_j, start_j, far_j, nexts_j, solved_j, sems_j),
    ):
        end_inward(line, ends, start, sems.at[0], far, sems.at[1])
        if line.half > 1:

            @pl.when(jnp.logical_not(line.end))
            def _():
                line.send(solved, nexts, sems.at[2], line.outer).wait_send()

    finish(rows_j, speeds, right, lines, spectral, filled, advanced, increment, *thirds)


def finish(
    rows_j, speeds, right, lines, spectral, filled,
    advanced, increment, values, coupling, gain_1, gain_2,
):
    variables, total, lanes = lines.shape
    rows_i = total // rows_j
    quarters = total // LANES
    per_quarter = LANES // rows_i
    depth = values.shape[0] // lanes

    for q in range(quarters):
        rho = jnp.concatenate(
            [
                spectral[2, pl.ds(q * per_quarter + j, rows_i, stride=rows_j), :]
                for j in range(per_quarter)
            ],
            axis=0,
        ).T
        for v in range(variables):
            at = pl.ds(v * quarters + q, lanes, stride=depth)
            coupling[at, :] = speeds[2 * variables + v] * rho
            values[at, :] = lines[v, q * LANES : (q + 1) * LANES, :].T
    for spare in range(variables * quarters, depth):
        at = pl.ds(spare, lanes, stride=depth)
        coupling[at, :] = jnp.zeros((lanes, lanes), F32)
        values[at, :] = jnp.zeros((lanes, lanes), F32)

    half = lanes // 2
    gain_1[:depth, :] = jnp.zeros((depth, lanes), F32)
    zero = gain_1[:depth, :]

    def ahead(n, carry):
        fresh = []
        for side in range(2):
            older_first, older_second, older, last_first, last_second, newer = carry[side]
            k = n if side == 0 else lanes - 1 - n
            at = pl.ds(pl.multiple_of(k * depth, BS), depth)
            inverse, coupled, one, two = eliminate(
                coupling[at, :], older_first, older_second, last_first, last_second
            )
            value = values[at, :] * inverse - two * older - coupled * newer
            gain_1[at, :] = one
            gain_2[at, :] = two
            values[at, :] = value
            fresh.append((last_first, last_second, newer, one, two, value))
        return tuple(fresh)

    low, high = lax.fori_loop(0, half, ahead, ((zero,) * 6,) * 2)

    def ends(side):
        return [side[0], side[1], side[3], side[4]], [side[2], side[5]]

    low_next = meet(*ends(low), *ends(high))
    high_next = meet(*ends(high), *ends(low))

    def back(step, carry):
        fresh = []
        for side in range(2):
            nearer, farther = carry[side]
            n = half - 1 - step
            k = n if side == 0 else lanes - 1 - n
            at = pl.ds(pl.multiple_of(k * depth, BS), depth)
            value = values[at, :] - gain_1[at, :] * nearer - gain_2[at, :] * farther
            values[at, :] = value
            fresh.append((value, nearer))
        return tuple(fresh)

    lax.fori_loop(0, half, back, (low_next, high_next))
    for q in range(quarters):
        solved = [values[pl.ds(u * quarters + q, lanes, stride=depth), :] for u in range(variables)]
        for v in range(variables):
            total_v = right[v * variables] * solved[0]
            for u in range(1, variables):
                total_v = total_v + right[v * variables + u] * solved[u]
            turned = total_v.T
            for j in range(per_quarter):
                at = pl.ds(q * per_quarter + j, rows_i, stride=rows_j)
                piece = turned[j * rows_i : (j + 1) * rows_i]
                increment[v, at, :] = piece
                advanced[v, at, :] = filled[v, at, :] + piece


def local(
    flow_state, spectral, wave_speed, left_map, right_map,
    donor_block, receiver_block, fringe_count, fringe_weight,
):
    variables, grids, rows_i, rows_j, rows_k = flow_state.shape
    assert grids == 1 and rows_k == LANES
    total = rows_i * rows_j
    devices, capacity = donor_block.shape[1:]
    slots = devices * capacity
    flow = flow_state.reshape(variables, total, rows_k)
    rho = spectral.reshape(3, total, rows_k)
    speeds = wave_speed.reshape(-1)
    left = left_map.reshape(-1)
    right = right_map.reshape(-1)
    packed_rows = -(-variables * BS // GROUPS) * BS
    field = shape(variables, total, rows_k)
    i_plane = (variables, rows_j, rows_k)
    j_plane = (variables, rows_i, rows_k)
    axes = ("ia", "ja", "ka")

    cube_count = total // (BS * BS) * (rows_k // BS)
    depth = -(-variables * (total // LANES) // BS) * BS
    live = jnp.arange(capacity, dtype=jnp.int32)[None, :] < fringe_count[0][:, None]
    target = jnp.where(live, receiver_block[0], -1).reshape(-1)
    slot = jnp.arange(slots, dtype=jnp.int32)
    hits = target[None, :] == jnp.arange(cube_count, dtype=jnp.int32)[:, None]
    source = jnp.max(jnp.where(hits, slot[None, :], -1), axis=1)
    dma = pltpu.SemaphoreType.DMA

    def held(*dims):
        return pltpu.VMEM(dims, F32)

    whole = [held(variables, total, rows_k)]
    advanced, increment = call(
        functools.partial(step_body, axes, capacity, rows_i, rows_j),
        [field, field],
        [SMEM] * 6 + [VMEM] * 2,
        (speeds, left, right, donor_block.reshape(-1), source, fringe_weight.reshape(-1), flow, rho),
        scratch=[
            held(cube_count, packed_rows, LANES),
            held(slots, packed_rows, LANES),
            held(slots, packed_rows, LANES),
        ]
        + whole
        + whole * 4
        + [held(4, *i_plane)] * 3
        + whole * 4
        + [held(4, *j_plane)] * 3
        + [dma((devices,))] * 2
        + [dma((2, 2))] * 2
        + [
            held(variables, total + 2 * rows_j, rows_k),
            *whole * 2,
            held(2, *i_plane),
            held(2, *j_plane),
            held(2, *j_plane),
            dma((2, 4)),
        ]
        + [held(2, *i_plane)] * 5
        + [dma((3, 2))]
        + [held(2, *j_plane)] * 5
        + [dma((3, 2))]
        + whole
        + [held(rows_k * depth, LANES)] * 4,
        collective_id=0,
    )
    return advanced.reshape(flow_state.shape), increment.reshape(flow_state.shape)


def solution(mesh):
    return jax.shard_map(
        local,
        mesh=mesh,
        in_specs=(
            P(None, "ka", "ia", "ja", None),
            P(None, "ka", "ia", "ja", None),
            P(None, "ka", None),
            P("ka", None, None),
            P("ka", None, None),
            P(("ia", "ja", "ka"), None, None),
            P(("ia", "ja", "ka"), None, None),
            P(("ia", "ja", "ka"), None),
            P(None, ("ia", "ja", "ka"), None, None),
        ),
        out_specs=(P(None, "ka", "ia", "ja", None), P(None, "ka", "ia", "ja", None)),
        check_vma=False,
    )
```

```python
import functools
import math

import jax
import jax.numpy as jnp
from jax import lax
from jax.experimental import pallas as pl
from jax.experimental.pallas import tpu as pltpu
from jax.sharding import PartitionSpec as P

BS = 8
LANES = 128
GROUPS = LANES // BS
QUARTER = 0.25
VMEM = pl.BlockSpec(memory_space=pltpu.VMEM)
SMEM = pl.BlockSpec(memory_space=pltpu.SMEM)
F32 = jnp.float32


def call(body, outs, ins, args, scratch=(), flops=4_000_000, collective_id=None):
    moved = sum(a.size * 4 for a in args) + sum(o.size * 4 for o in outs)
    held = sum(math.prod(r.shape) * 4 for r in scratch if math.prod(r.shape) > 1024)
    options = {} if collective_id is None else {"collective_id": collective_id, "has_side_effects": True}
    return pl.pallas_call(
        body,
        out_shape=outs,
        in_specs=ins,
        out_specs=[VMEM] * len(outs),
        scratch_shapes=list(scratch),
        compiler_params=pltpu.CompilerParams(vmem_limit_bytes=moved + held + (3 << 20), **options),
        cost_estimate=pl.CostEstimate(flops=flops, bytes_accessed=moved, transcendentals=0),
    )(*args)


def shape(*dims):
    return jax.ShapeDtypeStruct(dims, F32)


def lane_iota():
    return lax.broadcasted_iota(jnp.int32, (BS, LANES), 1)


def groups_turned(tiles):
    group = lane_iota() // BS
    tiles = list(tiles)
    distance = 1
    while distance < GROUPS:
        upper = (group // distance) % 2 == 1
        shift = distance * BS
        for a in range(GROUPS):
            if a & distance == 0:
                x, y = tiles[a], tiles[a + distance]
                tiles[a] = jnp.where(upper, pltpu.roll(y, shift, 1), x)
                tiles[a + distance] = jnp.where(upper, y, pltpu.roll(x, LANES - shift, 1))
        distance *= 2
    return tiles


def tile_at(block, rows_j, g):
    blocks_j = rows_j // BS
    row = (block // blocks_j) * (BS * rows_j) + (block % blocks_j) * BS + (g % BS) * rows_j
    return pl.ds(pl.multiple_of(row, BS), BS)


def pack_all(rows_j, flow, packed):
    groups = flow.shape[0] * BS

    def one(block, carry):
        for first in range(0, groups, GROUPS):
            count = min(GROUPS, groups - first)
            tiles = [flow[g // BS, tile_at(block, rows_j, g), :] for g in range(first, first + count)]
            tiles = groups_turned(tiles + tiles[:1] * (GROUPS - count))
            q = first // GROUPS
            for k in range(GROUPS):
                packed[block * GROUPS + k, q * BS : (q + 1) * BS, :] = tiles[k]
        return carry

    lax.fori_loop(0, packed.shape[0] // GROUPS, one, 0)


def unpack_all(rows_j, source, packed, arrived, filled):
    groups = filled.shape[0] * BS

    def one(block, carry):
        for first in range(0, groups, GROUPS):
            q = first // GROUPS
            tiles = []
            for k in range(GROUPS):
                slot = source[block * GROUPS + k]
                live = jnp.full((BS, LANES), slot, jnp.int32) >= 0
                fresh = arrived[jnp.maximum(slot, 0), q * BS : (q + 1) * BS, :]
                kept = packed[block * GROUPS + k, q * BS : (q + 1) * BS, :]
                tiles.append(jnp.where(live, fresh, kept))
            tiles = groups_turned(tiles)
            for g in range(first, min(first + GROUPS, groups)):
                filled[g // BS, tile_at(block, rows_j, g), :] = tiles[g - first]
        return carry

    lax.fori_loop(0, packed.shape[0] // GROUPS, one, 0)


def blend(cubes, shifted, weight):
    return (1.0 - weight) * cubes + weight * shifted


def interpolate_all(weights, arrived):
    slots, packed_rows, lanes = arrived.shape
    lane = lax.broadcasted_iota(jnp.int32, (packed_rows, LANES), 1)
    row = lax.broadcasted_iota(jnp.int32, (packed_rows, LANES), 0)

    def one(slot, carry):
        cubes = arrived[slot]
        after = jnp.where(lane % (BS * BS) >= BS * (BS - 1), cubes, pltpu.roll(cubes, LANES - BS, 1))
        cubes = blend(cubes, after, weights[slot])
        after = jnp.where(row % BS == BS - 1, cubes, pltpu.roll(cubes, packed_rows - 1, 0))
        cubes = blend(cubes, after, weights[slots + slot])
        after = jnp.where(lane % BS == BS - 1, cubes, pltpu.roll(cubes, LANES - 1, 1))
        arrived[slot] = blend(cubes, after, weights[2 * slots + slot])
        return carry

    lax.fori_loop(0, slots, one, 0, unroll=4)


def eliminate(coupling, older_first, older_second, last_first, last_second):
    fourth = QUARTER * coupling
    coupled = -coupling + fourth * older_first
    pivots = 1.0 + 2.5 * coupling + fourth * older_second - last_first * coupled
    inverse = 1.0 / pivots
    first = (-coupling - last_second * coupled) * inverse
    second = -fourth * inverse
    return inverse, coupled * inverse, first, second


def meet(gains, values, far_gains, far_values):
    f0, s0, f1, s1 = gains
    g0, t0, g1, t1 = far_gains
    r0, r1 = values
    q0, q1 = far_values
    cross = g1 - t1 * f0
    a11 = 1.0 - t1 * s0 - cross * f1
    a12 = -cross * s1
    b1 = q1 - t1 * r0 - cross * r1
    a21 = g0 - t0 * f1
    a22 = 1.0 - t0 * s1
    b2 = q0 - t0 * r1
    scale = 1.0 / (a11 * a22 - a12 * a21)
    return (b1 * a22 - a12 * b2) * scale, (a11 * b2 - a21 * b1) * scale


def row_of(n, count, lower):
    return jnp.where(lower, n, count - 1 - n)


def factor_pass(direction, rows, stride, is_lower, speeds, spectral, start, outs, last):
    inverse, coupled, first, second = outs
    variables, total, lanes = inverse.shape
    plane = total // rows

    def one(n, carry):
        row = row_of(n, rows, is_lower)
        at = pl.ds(pl.multiple_of(row * plane, BS), plane)
        if stride is None:
            rho = spectral[direction, at, :]
        else:
            rho = spectral[direction, pl.ds(row, plane, stride=stride), :]
        fresh = []
        for v in range(variables):
            older_first, older_second, last_first, last_second = carry[v]
            a, b, c, d = eliminate(
                speeds[direction * variables + v] * rho, older_first, older_second, last_first, last_second
            )
            inverse[v, at, :] = a
            coupled[v, at, :] = b
            first[v, at, :] = c
            second[v, at, :] = d
            fresh.append((last_first, last_second, c, d))
        return tuple(fresh)

    begin = tuple(tuple(start[m, v] for m in range(4)) for v in range(variables))
    ends = lax.fori_loop(0, rows, one, begin)
    for v in range(variables):
        for m in range(4):
            last[m, v] = ends[v][m]


class Line:
    def __init__(self, axis):
        self.axis = axis
        self.members = lax.axis_size(axis)
        self.half = self.members // 2
        self.place = lax.axis_index(axis)
        self.lower = self.place < self.half
        self.depth = jnp.where(self.lower, self.place, self.members - 1 - self.place)
        self.inner = jnp.where(self.lower, self.place + 1, self.place - 1)
        self.outer = jnp.where(self.lower, self.place - 1, self.place + 1)
        self.middle = self.depth == self.half - 1
        self.end = self.depth == 0

    def send(self, source, target, sems, device):
        return pltpu.make_async_remote_copy(
            src_ref=source,
            dst_ref=target,
            send_sem=sems.at[0],
            recv_sem=sems.at[1],
            device_id={self.axis: device},
            device_id_type=pl.DeviceIdType.MESH,
        )


def take_start(line, source, start, sems):
    @pl.when(line.end)
    def _():
        start[...] = jnp.zeros(start.shape, F32)

    if line.half > 1:

        @pl.when(jnp.logical_not(line.end))
        def _():
            line.send(source, start, sems, line.inner).wait_recv()


def send_inward(line, source, start, start_sems, far, far_sems):
    if line.half > 1:

        @pl.when(jnp.logical_not(line.middle))
        def _():
            line.send(source, start, start_sems, line.inner).start()

    @pl.when(line.middle)
    def _():
        line.send(source, far, far_sems, line.inner).start()


def end_inward(line, source, start, start_sems, far, far_sems):
    if line.half > 1:

        @pl.when(jnp.logical_not(line.middle))
        def _():
            line.send(source, start, start_sems, line.inner).wait_send()

    @pl.when(line.middle)
    def _():
        line.send(source, far, far_sems, line.inner).wait_send()


def peer_of(number, axes):
    rest, place = number, {}
    for axis in reversed(axes):
        place[axis] = rest % lax.axis_size(axis)
        rest = rest // lax.axis_size(axis)
    return place


def residual_pass(
    rows_i, is_lower, left, padded, spectral, j_before, j_after, inverse, coupled, second, start, reduced, last
):
    variables, total, lanes = inverse.shape
    rows_j = total // rows_i
    lane = lax.broadcasted_iota(jnp.int32, (rows_j, lanes), 1)
    row_id = lax.broadcasted_iota(jnp.int32, (rows_j, lanes), 0)

    def one(n, carry):
        row = row_of(n, rows_i, is_lower)
        base = pl.multiple_of(row * rows_j, BS)
        at = pl.ds(base, rows_j)
        rho = [spectral[e, at, :] for e in range(3)]
        residual = []
        for v in range(variables):
            center = padded[v, pl.ds(base + rows_j, rows_j), :]
            twice = 2.0 * center
            along_i = padded[v, pl.ds(base + 2 * rows_j, rows_j), :] + padded[v, at, :] - twice
            after = jnp.where(
                row_id == rows_j - 1, j_after[v, pl.ds(row, 1), :], pltpu.roll(center, rows_j - 1, 0)
            )
            before = jnp.where(row_id == 0, j_before[v, pl.ds(row, 1), :], pltpu.roll(center, 1, 0))
            along_j = after + before - twice
            after = jnp.where(lane == lanes - 1, 0.0, pltpu.roll(center, lanes - 1, 1))
            before = jnp.where(lane == 0, 0.0, pltpu.roll(center, 1, 1))
            along_k = after + before - twice
            residual.append(rho[0] * along_i + rho[1] * along_j + rho[2] * along_k)
        fresh = []
        for v in range(variables):
            source = left[v * variables] * residual[0]
            for u in range(1, variables):
                source = source + left[v * variables + u] * residual[u]
            older, newer = carry[v]
            value = source * inverse[v, at, :] - second[v, at, :] * older - coupled[v, at, :] * newer
            reduced[v, at, :] = value
            fresh.append((newer, value))
        return tuple(fresh)

    ends = lax.fori_loop(0, rows_i, one, begin_of(start, variables))
    for v in range(variables):
        last[0, v] = ends[v][0]
        last[1, v] = ends[v][1]


def forward_pass(rows, is_lower, source, inverse, coupled, second, start, reduced, last):
    variables, total, lanes = source.shape
    plane = total // rows

    def one(n, carry):
        at = pl.ds(pl.multiple_of(row_of(n, rows, is_lower) * plane, BS), plane)
        fresh = []
        for v in range(variables):
            older, newer = carry[v]
            value = (
                source[v, at, :] * inverse[v, at, :]
                - second[v, at, :] * older
                - coupled[v, at, :] * newer
            )
            reduced[v, at, :] = value
            fresh.append((newer, value))
        return tuple(fresh)

    begin = tuple((start[0, v], start[1, v]) for v in range(variables))
    ends = lax.fori_loop(0, rows, one, begin)
    for v in range(variables):
        last[0, v] = ends[v][0]
        last[1, v] = ends[v][1]


def backward_pass(rows, is_lower, reduced, first, second, begin, store):
    variables, total, lanes = reduced.shape
    plane = total // rows

    def one(step, carry):
        row = row_of(rows - 1 - step, rows, is_lower)
        at = pl.ds(pl.multiple_of(row * plane, BS), plane)
        fresh = []
        for v in range(variables):
            nearer, farther = carry[v]
            value = reduced[v, at, :] - first[v, at, :] * nearer - second[v, at, :] * farther
            store(v, row, value)
            fresh.append((value, nearer))
        return tuple(fresh)

    return lax.fori_loop(0, rows, one, begin)


def start_values(variables, gains, values, far_gains, far_values):
    return tuple(
        meet(
            [gains[m, v] for m in range(4)],
            [values[m, v] for m in range(2)],
            [far_gains[m, v] for m in range(4)],
            [far_values[m, v] for m in range(2)],
        )
        for v in range(variables)
    )


def begin_of(next_values, variables):
    return tuple((next_values[0, v], next_values[1, v]) for v in range(variables))


def solve_back(line, rows, reduced, gains, last_gains, far_gains, last, far, far_sems, nexts, next_sems, solved, store):
    variables = reduced.shape[0]

    @pl.when(line.middle)
    def _():
        line.send(last, far, far_sems, line.inner).wait_recv()
        for v, pair in enumerate(start_values(variables, last_gains, last, far_gains, far)):
            nexts[0, v] = pair[0]
            nexts[1, v] = pair[1]

    if line.half > 1:

        @pl.when(jnp.logical_not(line.middle))
        def _():
            line.send(solved, nexts, next_sems, line.outer).wait_recv()

    ends = backward_pass(
        rows, line.lower, reduced, gains[2], gains[3], begin_of(nexts, variables), store
    )
    if line.half > 1:
        for v in range(variables):
            solved[0, v] = ends[v][0]
            solved[1, v] = ends[v][1]

        @pl.when(jnp.logical_not(line.end))
        def _():
            line.send(solved, nexts, next_sems, line.outer).start()


def step_body(
    axes, capacity, rows_i, rows_j, speeds, left, right, donor, source, weights, flow, spectral,
    advanced, increment, *refs,
):
    packed, outbound, arrived, filled = refs[:4]
    gains_i, (last_gains_i, far_gains_i, start_gains_i) = refs[4:8], refs[8:11]
    gains_j, (last_gains_j, far_gains_j, start_gains_j) = refs[11:15], refs[15:18]
    sent, got, gain_sems_i, gain_sems_j = refs[18:22]
    (padded, reduced, turned, i_halo, j_edge, j_halo, halo_sems) = refs[22:29]
    ends_i, start_i, far_i, nexts_i, solved_i, sems_i = refs[29:35]
    ends_j, start_j, far_j, nexts_j, solved_j, sems_j = refs[35:41]
    lines, thirds = refs[41], refs[42:]
    variables, total, lanes = flow.shape
    line_i, line_j = Line("ia"), Line("ja")
    devices = 1
    me = 0
    for axis in axes:
        devices = devices * lax.axis_size(axis)
        me = me * lax.axis_size(axis) + lax.axis_index(axis)
    barrier = pltpu.get_barrier_semaphore()

    def greet(step, carry):
        peer = peer_of((me + step) % devices, axes)
        pl.semaphore_signal(barrier, inc=1, device_id=peer, device_id_type=pl.DeviceIdType.MESH)
        return carry

    lax.fori_loop(1, devices, greet, 0)
    pack_all(rows_j, flow, packed)

    def gather(slot, carry):
        outbound[slot] = packed[donor[slot]]
        return carry

    lax.fori_loop(0, devices * capacity, gather, 0, unroll=4)
    pl.semaphore_wait(barrier, devices - 1)

    def slots(device):
        return pl.ds(device * capacity, capacity)

    def cubes(step, to, of):
        return pltpu.make_async_remote_copy(
            src_ref=outbound.at[slots(to)],
            dst_ref=arrived.at[slots(of)],
            send_sem=sent.at[step],
            recv_sem=got.at[step],
            device_id=peer_of(to, axes),
            device_id_type=pl.DeviceIdType.MESH,
        )

    def begin(step, carry):
        cubes(step, (me + step) % devices, me).start()
        return carry

    lax.fori_loop(1, devices, begin, 0)
    arrived[slots(me)] = outbound[slots(me)]

    for direction, line, rows, stride, gains, last, far, start, sems in (
        (1, line_j, rows_j, rows_j, gains_j, last_gains_j, far_gains_j, start_gains_j, gain_sems_j),
        (0, line_i, rows_i, None, gains_i, last_gains_i, far_gains_i, start_gains_i, gain_sems_i),
    ):
        take_start(line, last, start, sems.at[0])
        factor_pass(direction, rows, stride, line.lower, speeds, spectral, start, gains, last)
        send_inward(line, last, start, sems.at[0], far, sems.at[1])

    factor_third(rows_j, total, speeds, spectral, *thirds[:6])

    def end(step, carry):
        cubes(step, (me + step) % devices, (me + devices - step) % devices).wait_recv()
        return carry

    lax.fori_loop(1, devices, end, 0)
    interpolate_all(weights, arrived)
    unpack_all(rows_j, source, packed, arrived, filled)

    def sides(line):
        return (line.place > 0, line.place - 1), (line.place < line.members - 1, line.place + 1)

    for v in range(variables):
        j_edge[0, v] = filled[v, pl.ds(0, rows_i, stride=rows_j), :]
        j_edge[1, v] = filled[v, pl.ds(rows_j - 1, rows_i, stride=rows_j), :]
    def edges(axis_number, side):
        if axis_number == 1:
            return j_edge.at[side], j_halo.at[1 - side]
        first = 0 if side == 0 else total - rows_j
        return filled.at[:, pl.ds(first, rows_j), :], i_halo.at[1 - side]

    def halo(line, axis_number, side, device):
        source, target = edges(axis_number, side)
        number = axis_number * 2 + side
        return pltpu.make_async_remote_copy(
            src_ref=source,
            dst_ref=target,
            send_sem=halo_sems.at[0, number],
            recv_sem=halo_sems.at[1, number],
            device_id={line.axis: device},
            device_id_type=pl.DeviceIdType.MESH,
        )

    for axis_number, line in ((1, line_j), (0, line_i)):
        for side, (there, device) in enumerate(sides(line)):

            @pl.when(there)
            def _():
                halo(line, axis_number, side, device).start()

    padded[:, rows_j : rows_j + total, :] = filled[...]
    for axis_number, line in ((0, line_i), (1, line_j)):
        for side, (there, device) in enumerate(sides(line)):
            target = (i_halo, j_halo)[axis_number]

            @pl.when(there)
            def _():
                halo(line, axis_number, 1 - side, device).wait_recv()

            @pl.when(jnp.logical_not(there))
            def _():
                target[side] = jnp.zeros(target.shape[1:], F32)

    padded[:, :rows_j, :] = i_halo[0]
    padded[:, rows_j + total :, :] = i_halo[1]

    take_start(line_i, ends_i, start_i, sems_i.at[0])
    residual_pass(
        rows_i, line_i.lower, left, padded, spectral, j_halo.at[0], j_halo.at[1],
        gains_i[0], gains_i[1], gains_i[3], start_i, reduced, ends_i,
    )
    send_inward(line_i, ends_i, start_i, sems_i.at[0], far_i, sems_i.at[1])

    def store_turned(v, row, value):
        turned[v, pl.ds(row, rows_j, stride=rows_i), :] = value

    @pl.when(line_i.middle)
    def _():
        line_i.send(last_gains_i, far_gains_i, gain_sems_i.at[1], line_i.inner).wait_recv()

    solve_back(
        line_i, rows_i, reduced, gains_i, last_gains_i, far_gains_i, ends_i, far_i, sems_i.at[1],
        nexts_i, sems_i.at[2], solved_i, store_turned,
    )

    take_start(line_j, ends_j, start_j, sems_j.at[0])
    forward_pass(
        rows_j, line_j.lower, turned, gains_j[0], gains_j[1], gains_j[3], start_j, reduced, ends_j
    )
    send_inward(line_j, ends_j, start_j, sems_j.at[0], far_j, sems_j.at[1])

    def store_lines(v, row, value):
        lines[v, pl.ds(pl.multiple_of(row * rows_i, BS), rows_i), :] = value

    @pl.when(line_j.middle)
    def _():
        line_j.send(last_gains_j, far_gains_j, gain_sems_j.at[1], line_j.inner).wait_recv()

    solve_back(
        line_j, rows_j, reduced, gains_j, last_gains_j, far_gains_j, ends_j, far_j, sems_j.at[1],
        nexts_j, sems_j.at[2], solved_j, store_lines,
    )

    for axis_number, line in ((0, line_i), (1, line_j)):
        for side, (there, device) in enumerate(sides(line)):

            @pl.when(there)
            def _():
                halo(line, axis_number, side, device).wait_send()

    def close(step, carry):
        cubes(step, (me + step) % devices, me).wait_send()
        return carry

    lax.fori_loop(1, devices, close, 0)
    end_inward(line_i, last_gains_i, start_gains_i, gain_sems_i.at[0], far_gains_i, gain_sems_i.at[1])
    end_inward(line_j, last_gains_j, start_gains_j, gain_sems_j.at[0], far_gains_j, gain_sems_j.at[1])
    for line, ends, start, far, nexts, solved, sems in (
        (line_i, ends_i, start_i, far_i, nexts_i, solved_i, sems_i),
        (line_j, ends_j, start_j, far_j, nexts_j, solved_j, sems_j),
    ):
        end_inward(line, ends, start, sems.at[0], far, sems.at[1])
        if line.half > 1:

            @pl.when(jnp.logical_not(line.end))
            def _():
                line.send(solved, nexts, sems.at[2], line.outer).wait_send()

    finish(rows_j, right, lines, filled, advanced, increment, *thirds)


def turned_rows(quarter, quarters, v, lanes, depth):
    return pl.ds(v * quarters + quarter, lanes, stride=depth)


def both_ends(n, lanes, depth):
    return [pl.ds(pl.multiple_of(k * depth, BS), depth) for k in (n, lanes - 1 - n)]


def factor_third(rows_j, total, speeds, spectral, values, inverse, coupled, gain_1, gain_2, last):
    lanes = spectral.shape[2]
    rows_i = total // rows_j
    quarters = total // LANES
    per_quarter = LANES // rows_i
    depth = values.shape[0] // lanes
    count = speeds.shape[0] // 3
    for q in range(quarters):
        rho = jnp.concatenate(
            [
                spectral[2, pl.ds(q * per_quarter + j, rows_i, stride=rows_j), :]
                for j in range(per_quarter)
            ],
            axis=0,
        ).T
        for v in range(count):
            inverse[turned_rows(q, quarters, v, lanes, depth), :] = speeds[2 * count + v] * rho
    for spare in range(count * quarters, depth):
        at = pl.ds(spare, lanes, stride=depth)
        inverse[at, :] = jnp.zeros((lanes, lanes), F32)
        values[at, :] = jnp.zeros((lanes, lanes), F32)

    last[...] = jnp.zeros(last.shape, F32)
    begin = tuple(tuple(last[side, m] for m in range(4)) for side in range(2))

    def one(n, carry):
        fresh = []
        for side, at in enumerate(both_ends(n, lanes, depth)):
            older_first, older_second, last_first, last_second = carry[side]
            a, b, c, d = eliminate(inverse[at, :], older_first, older_second, last_first, last_second)
            inverse[at, :] = a
            coupled[at, :] = b
            gain_1[at, :] = c
            gain_2[at, :] = d
            fresh.append((last_first, last_second, c, d))
        return tuple(fresh)

    ends = lax.fori_loop(0, lanes // 2, one, begin)
    for side in range(2):
        for m in range(4):
            last[side, m] = ends[side][m]


def finish(
    rows_j, right, lines, filled, advanced, increment, values, inverse, coupled, gain_1, gain_2, last, carry
):
    variables, total, lanes = lines.shape
    rows_i = total // rows_j
    quarters = total // LANES
    per_quarter = LANES // rows_i
    depth = values.shape[0] // lanes
    for q in range(quarters):
        for v in range(variables):
            at = turned_rows(q, quarters, v, lanes, depth)
            values[at, :] = lines[v, q * LANES : (q + 1) * LANES, :].T

    half = lanes // 2
    carry[...] = jnp.zeros(carry.shape, F32)

    def ahead(n, state):
        fresh = []
        for side, at in enumerate(both_ends(n, lanes, depth)):
            older, newer = state[side]
            value = values[at, :] * inverse[at, :] - gain_2[at, :] * older - coupled[at, :] * newer
            values[at, :] = value
            fresh.append((newer, value))
        return tuple(fresh)

    begin = tuple((carry[side, 0], carry[side, 1]) for side in range(2))
    low, high = lax.fori_loop(0, half, ahead, begin, unroll=2)
    gains = [[last[side, m] for m in range(4)] for side in range(2)]
    low_next = meet(gains[0], low, gains[1], high)
    high_next = meet(gains[1], high, gains[0], low)

    def back(step, state):
        fresh = []
        for side, at in enumerate(both_ends(half - 1 - step, lanes, depth)):
            nearer, farther = state[side]
            value = values[at, :] - gain_1[at, :] * nearer - gain_2[at, :] * farther
            values[at, :] = value
            fresh.append((value, nearer))
        return tuple(fresh)

    lax.fori_loop(0, half, back, (low_next, high_next), unroll=2)
    for q in range(quarters):
        solved = [values[turned_rows(q, quarters, u, lanes, depth), :] for u in range(variables)]
        for v in range(variables):
            total_v = right[v * variables] * solved[0]
            for u in range(1, variables):
                total_v = total_v + right[v * variables + u] * solved[u]
            turned = total_v.T
            for j in range(per_quarter):
                at = pl.ds(q * per_quarter + j, rows_i, stride=rows_j)
                piece = turned[j * rows_i : (j + 1) * rows_i]
                increment[v, at, :] = piece
                advanced[v, at, :] = filled[v, at, :] + piece


def local(
    flow_state, spectral, wave_speed, left_map, right_map,
    donor_block, receiver_block, fringe_count, fringe_weight,
):
    variables, grids, rows_i, rows_j, rows_k = flow_state.shape
    assert grids == 1 and rows_k == LANES
    total = rows_i * rows_j
    devices, capacity = donor_block.shape[1:]
    slots = devices * capacity
    flow = flow_state.reshape(variables, total, rows_k)
    rho = spectral.reshape(3, total, rows_k)
    speeds = wave_speed.reshape(-1)
    left = left_map.reshape(-1)
    right = right_map.reshape(-1)
    packed_rows = -(-variables * BS // GROUPS) * BS
    field = shape(variables, total, rows_k)
    i_plane = (variables, rows_j, rows_k)
    j_plane = (variables, rows_i, rows_k)
    axes = ("ia", "ja", "ka")

    cube_count = total // (BS * BS) * (rows_k // BS)
    depth = -(-variables * (total // LANES) // BS) * BS
    live = jnp.arange(capacity, dtype=jnp.int32)[None, :] < fringe_count[0][:, None]
    target = jnp.where(live, receiver_block[0], -1).reshape(-1)
    slot = jnp.arange(slots, dtype=jnp.int32)
    hits = target[None, :] == jnp.arange(cube_count, dtype=jnp.int32)[:, None]
    source = jnp.max(jnp.where(hits, slot[None, :], -1), axis=1)
    dma = pltpu.SemaphoreType.DMA

    def held(*dims):
        return pltpu.VMEM(dims, F32)

    whole = [held(variables, total, rows_k)]
    advanced, increment = call(
        functools.partial(step_body, axes, capacity, rows_i, rows_j),
        [field, field],
        [SMEM] * 6 + [VMEM] * 2,
        (speeds, left, right, donor_block.reshape(-1), source, fringe_weight.reshape(-1), flow, rho),
        scratch=[
            held(cube_count, packed_rows, LANES),
            held(slots, packed_rows, LANES),
            held(slots, packed_rows, LANES),
        ]
        + whole
        + whole * 4
        + [held(4, *i_plane)] * 3
        + whole * 4
        + [held(4, *j_plane)] * 3
        + [dma((devices,))] * 2
        + [dma((2, 2))] * 2
        + [
            held(variables, total + 2 * rows_j, rows_k),
            *whole * 2,
            held(2, *i_plane),
            held(2, *j_plane),
            held(2, *j_plane),
            dma((2, 4)),
        ]
        + [held(2, *i_plane)] * 5
        + [dma((3, 2))]
        + [held(2, *j_plane)] * 5
        + [dma((3, 2))]
        + whole
        + [held(rows_k * depth, LANES)] * 5
        + [held(2, 4, depth, LANES), held(2, 2, depth, LANES)],
        collective_id=0,
    )
    return advanced.reshape(flow_state.shape), increment.reshape(flow_state.shape)


def solution(mesh):
    return jax.shard_map(
        local,
        mesh=mesh,
        in_specs=(
            P(None, "ka", "ia", "ja", None),
            P(None, "ka", "ia", "ja", None),
            P(None, "ka", None),
            P("ka", None, None),
            P("ka", None, None),
            P(("ia", "ja", "ka"), None, None),
            P(("ia", "ja", "ka"), None, None),
            P(("ia", "ja", "ka"), None),
            P(None, ("ia", "ja", "ka"), None, None),
        ),
        out_specs=(P(None, "ka", "ia", "ja", None), P(None, "ka", "ia", "ja", None)),
        check_vma=False,
    )
```
